32 devices in a mesh: groups: 2 (over y), expert: 4 (over z), dp: 4 (over x, core).
Axes of the slice: x: 2, y: 2, z: 4, core: 2. Of those that a mesh axis runs over, the one named last changes fastest.
Arguments:
- tokens: bfloat16 [4096, 2048], P(('groups', 'expert', 'dp')), parts along dimension 0, may hold values from -6 to 6
- cotangent: bfloat16 [4096, 2048], P(('groups', 'expert', 'dp')), parts along dimension 0, may hold values from -1.5 to 1.5
- expert_ids: int32 [4096, 8], P(('groups', 'expert', 'dp')), parts along dimension 0, may hold values from 0 to 127, all different within a row; in each aligned block of 128 rows (0 to 127, 128 to 255, ...) at most 16 rows name the same one
- gate_probs: float32 [4096, 8], P(('groups', 'expert', 'dp')), parts along dimension 0, may hold values from 0.05 to 0.6
- w_gate: bfloat16 [4, 2048, 384], P('expert', 'dp'), may hold values from -0.125 to 0.125
- w_up: bfloat16 [4, 2048, 384], P('expert', 'dp'), may hold values from -0.125 to 0.125
- w_down: bfloat16 [4, 384, 2048], P('expert', None, 'dp'), may hold values from -0.3125 to 0.3125
Outputs:
- mixed: bfloat16 [4096, 2048], P(('groups', 'expert', 'dp')), parts along dimension 0
- grad_tokens: bfloat16 [4096, 2048], P(('groups', 'expert', 'dp')), parts along dimension 0
- grad_gates: float32 [4096, 8], P(('groups', 'expert', 'dp')), parts along dimension 0
- grad_w_gate: bfloat16 [8, 2048, 384], P(('groups', 'expert'), 'dp'), parts along dimension 0
- grad_w_up: bfloat16 [8, 2048, 384], P(('groups', 'expert'), 'dp'), parts along dimension 0
- grad_w_down: bfloat16 [8, 384, 2048], P(('groups', 'expert'), None, 'dp'), parts along dimension 0
The draws below stay inside these ranges and needn't reach their ends.
There are 2 independent parts, one for each index of `groups`. The reference program is written for one: setup_inputs(seed, part) draws one part's arguments, and reference() takes and returns one part's arrays. A program takes and returns all parts, laid end to end along the dimension named above; an argument that names none is the same for every part. Nothing has to cross between parts.
Inputs may be any that keep to these rules, and one draw needn't show every extreme that they name: `expert_ids`: each token names 8 different experts. In the rows of one device (aligned blocks of 128 tokens) no expert is named more than 16 times, and in every draw some expert is named exactly 16 times in some block.
All inputs are finite; a program needn't handle non-finite values.
Results may differ from the reference program's by a relative error of at most 0.0058.
Values may be sent and summed in bfloat16 or wider, within the bound.
No kernel may reach another device: no remote copies, remote signals or barrier semaphores. Data moves between devices by JAX's collectives and lax.ppermute only.
A program may use at most 128 MiB of HBM per device.

```python
import math
import jax
import jax.numpy as jnp
import numpy as np
from jax import lax

D = 2048
EXPERTS = 128
TOP = 8
FF = 384
TOK_DEV = 128
TOKENS = 2048
WAVE = 4
CAP = 16
N_EXPERT = 4
N_DP = 4


def steps_of(own_key, shape, cuts, low, top_value):
    loudness = 1.0
    for position, shards_of in cuts:
        steps = jax.random.uniform(jax.random.fold_in(jax.random.fold_in(own_key, 6), position), (shards_of,), jnp.float32, low / len(cuts), top_value / len(cuts))
        loudness = loudness * jnp.repeat(jnp.exp(steps), shape[position] // shards_of).reshape((-1,) + (1,) * (len(shape) - 1 - position))
    return loudness


def deal_out(rng, own, number, rows, number_of, top, limit, skew):
    ranking = jax.random.permutation(rng, number_of)
    heavy_load, common = portions_of(number_of, rows * top, limit, skew, True), portions_of(number_of, rows * top, limit, skew, False)
    places = jnp.arange(number_of)

    def named(lengths, offset_by):
        used = int((lengths > 0).sum())
        fixed = max(1, used // 4)
        shifted = fixed + (places - fixed + offset_by * (used - fixed)) % max(1, number_of - fixed)
        return jnp.zeros((number_of,), jnp.int32).at[ranking[jnp.where(places < fixed, places, shifted)]].set(jnp.asarray(lengths, jnp.int32))

    lengths = jnp.where(number % 4 == 0, named(heavy_load, number // 4), named(common, number - number // 4 - 1))
    mixed = jax.random.permutation(jax.random.fold_in(own, 3), number_of)
    donor, receiver = mixed[0:number_of // 2 * 2:2], mixed[1:number_of // 2 * 2:2]
    room = jnp.minimum(lengths[donor] - 1, limit - lengths[receiver]) // 2
    room = jnp.where((donor == ranking[0]) | (receiver == ranking[0]) | (lengths[receiver] == 0), 0, jnp.maximum(room, 0))
    shifted = jax.random.randint(jax.random.fold_in(own, 4), (number_of // 2,), 0, 1 << 20) % (room + 1)
    lengths = lengths.at[donor].add(-shifted).at[receiver].add(shifted)
    items = jnp.searchsorted(jnp.cumsum(lengths), jnp.arange(rows * top), side="right").astype(jnp.int32)
    grid = items.reshape(top, rows).T
    grid = grid[jax.random.permutation(jax.random.fold_in(own, 1), rows)]
    offset_by = jax.random.randint(jax.random.fold_in(own, 2), (rows, 1), 0, top)
    return jnp.take_along_axis(grid, (jnp.arange(top)[None, :] + offset_by) % top, axis=1)


def portions_of(count, total, most, skew, full):
    portions = [(1 << 20) // math.isqrt(standing ** skew) + 1 for standing in range(1, count + 1)]
    largest = most if full else min(most, max(-(-total // count), total * portions[0] // sum(portions)))
    least = 1 if total - largest >= count - 1 else 0
    given, surplus = [largest] + [least] * (count - 1), total - largest - least * (count - 1)
    while surplus > 0:
        free = [i for i in range(1, count) if given[i] < largest] or [i for i in range(1, count) if given[i] < most]
        pool, remaining = sum([portions[i] for i in free]), surplus
        for i in free:
            more = min(most - given[i], max(1, remaining * portions[i] // pool), surplus)
            given[i] = given[i] + more
            surplus = surplus - more
    return np.array(given)


def normal_values(stream_key, extent, deviation, reach, shards=(), held_as=jnp.bfloat16):
    array = deviation * jax.random.normal(stream_key, extent, jnp.float32)
    if shards:
        array = array * steps_of(stream_key, extent, shards, -0.22, 0.18)
    return jnp.clip(array, -reach, reach).astype(held_as)


def setup_inputs(seed: int = 0, part: int = 0) -> dict:
    keys = jax.random.split(jax.random.key(seed), 8)
    own_keys = jax.random.split(jax.random.fold_in(keys[7], part), 8)
    tokens = normal_values(own_keys[0], (TOKENS, D), 1.0, 6.0, ((0, 16),))
    cotangent = normal_values(own_keys[1], (TOKENS, D), 0.25, 1.5, ((0, 16),))
    expert_ids_keys = jax.random.split(jax.random.fold_in(own_keys[2], 1), TOKENS // TOK_DEV)
    expert_ids_turns = jax.random.permutation(jax.random.fold_in(own_keys[2], 3), TOKENS // TOK_DEV)
    expert_ids = jax.vmap(lambda own, number: deal_out(jax.random.fold_in(own_keys[2], 2), own, number, TOK_DEV, EXPERTS, TOP, CAP, 2))(expert_ids_keys, expert_ids_turns).reshape((TOKENS, TOP))
    gate_probs = jnp.clip(jnp.exp(math.log(0.6) - 2.4849067 * jax.random.uniform(own_keys[3], (TOKENS, TOP), jnp.float32) ** steps_of(own_keys[3], (TOKENS, TOP), ((0, 16),), -0.2, 0.2)), 0.05, 0.6)
    w_gate = normal_values(keys[4], (WAVE, D, FF), D ** -0.5, 0.125, ((0, 4), (1, 4)))
    w_up = normal_values(keys[5], (WAVE, D, FF), D ** -0.5, 0.125, ((0, 4), (1, 4)))
    w_down = normal_values(keys[6], (WAVE, FF, D), FF ** -0.5, 0.3125, ((0, 4), (2, 4)))
    return dict(tokens=tokens, cotangent=cotangent, expert_ids=expert_ids, gate_probs=gate_probs, w_gate=w_gate, w_up=w_up, w_down=w_down)


def expert_rows(rows_x, rows_dy, gate_full, up_full, down_full):
    gate_part = jnp.dot(rows_x, gate_full, preferred_element_type=jnp.float32)
    up_part = jnp.dot(rows_x, up_full, preferred_element_type=jnp.float32)
    sigmoid_gate = jax.nn.sigmoid(gate_part)
    activated = gate_part * sigmoid_gate
    hidden = (activated * up_part).astype(jnp.bfloat16)
    expert_out = jnp.dot(hidden, down_full, preferred_element_type=jnp.float32).astype(jnp.bfloat16)
    back_hidden = jnp.dot(rows_dy, down_full.T, preferred_element_type=jnp.float32)
    d_gate = (back_hidden * up_part * sigmoid_gate * (1.0 + gate_part * (1.0 - sigmoid_gate))).astype(jnp.bfloat16)
    d_up = (back_hidden * activated).astype(jnp.bfloat16)
    d_rows = (jnp.dot(d_gate, gate_full.T, preferred_element_type=jnp.float32)
              + jnp.dot(d_up, up_full.T, preferred_element_type=jnp.float32)).astype(jnp.bfloat16)
    return hidden, expert_out, d_gate, d_up, d_rows


def partial_sums(left_rows, right_rows):
    left_wide = left_rows.reshape(N_EXPERT, N_DP, CAP, left_rows.shape[1]).astype(jnp.float32)
    right_wide = right_rows.reshape(N_EXPERT, N_DP, CAP, right_rows.shape[1]).astype(jnp.float32)
    parts = jnp.einsum("epcd,epcf->pdf", left_wide, right_wide).astype(jnp.bfloat16)
    parts = lax.optimization_barrier(parts)
    return jnp.sum(parts.astype(jnp.float32), axis=0).astype(jnp.bfloat16)


def reference(tokens, cotangent, expert_ids, gate_probs, w_gate, w_up, w_down):
    blocks = N_EXPERT * N_DP
    block_ids = expert_ids.reshape(blocks, TOK_DEV * TOP)
    onehot = (block_ids[:, :, None] == jnp.arange(EXPERTS, dtype=jnp.int32)[None, None, :]).astype(jnp.int32)
    running = jnp.cumsum(onehot, axis=1)
    slot_index = (jnp.sum(running * onehot, axis=2) - 1).reshape(-1).astype(jnp.int32)
    flat_ids = expert_ids.reshape(-1)
    entry_index = jnp.arange(TOKENS * TOP, dtype=jnp.int32)
    token_index = entry_index // TOP
    top_index = entry_index % TOP
    block_index = token_index // TOK_DEV
    in_wave = flat_ids < WAVE
    row_index = block_index * CAP + slot_index
    expert_row = jnp.where(in_wave, flat_ids, WAVE).astype(jnp.int32)
    empty_table = jnp.full((WAVE, blocks * CAP), TOKENS, dtype=jnp.int32)
    table_token = empty_table.at[expert_row, row_index].set(token_index, mode="drop")
    table_top = jnp.zeros((WAVE, blocks * CAP), jnp.int32).at[expert_row, row_index].set(top_index, mode="drop")

    def per_expert(state_sums, inputs):
        mixed_sum, grad_sum, gate_grad = state_sums
        token_row, top_row, gate_full, up_full, down_full = inputs
        valid_row = token_row < TOKENS
        safe_row = jnp.minimum(token_row, TOKENS - 1).astype(jnp.int32)
        rows_x = jnp.where(valid_row[:, None], tokens[safe_row], jnp.zeros((), tokens.dtype))
        rows_dy = jnp.where(valid_row[:, None], cotangent[safe_row], jnp.zeros((), cotangent.dtype))
        hidden, expert_out, d_gate, d_up, d_rows = expert_rows(rows_x, rows_dy, gate_full, up_full, down_full)
        weight = jnp.where(valid_row, gate_probs[safe_row, top_row], jnp.zeros((), gate_probs.dtype))
        out_wide = expert_out.astype(jnp.float32)
        mixed_sum = mixed_sum.at[safe_row].add(weight[:, None] * out_wide)
        grad_sum = grad_sum.at[safe_row].add(weight[:, None] * d_rows.astype(jnp.float32))
        inner_prod = jnp.sum(rows_dy.astype(jnp.float32) * out_wide, axis=1)
        gate_grad = gate_grad.at[safe_row, top_row].add(jnp.where(valid_row, inner_prod, jnp.zeros((), inner_prod.dtype)))
        grad_gate_w = partial_sums(rows_x, d_gate)
        grad_up_w = partial_sums(rows_x, d_up)
        grad_down_w = partial_sums(hidden, rows_dy)
        return (mixed_sum, grad_sum, gate_grad), (grad_gate_w, grad_up_w, grad_down_w)

    start_sums = (jnp.zeros((TOKENS, D), jnp.float32), jnp.zeros((TOKENS, D), jnp.float32),
                  jnp.zeros((TOKENS, TOP), jnp.float32))
    final_sums, grads = lax.scan(per_expert, start_sums, (table_token, table_top, w_gate, w_up, w_down))
    mixed_sum, grad_sum, gate_grad = final_sums
    return (mixed_sum.astype(jnp.bfloat16), grad_sum.astype(jnp.bfloat16), gate_grad,
            grads[0], grads[1], grads[2])
```

```python
import jax
import jax.numpy as jnp
from jax import lax
from jax.sharding import PartitionSpec as P

EXPERTS = 128
CORES = 2


def dot_first(left, right):
    return lax.dot_general(
        left, right, (((0,), (0,)), ((), ())), preferred_element_type=jnp.float32
    )


def dot_last(left, right):
    return lax.dot_general(
        left, right, (((1,), (1,)), ((), ())), preferred_element_type=jnp.float32
    )


def dot(left, right):
    return jnp.dot(left, right, preferred_element_type=jnp.float32)


def on_device(tokens, cotangent, expert_ids, gate_probs, w_gate, w_up, w_down):
    expert_count = lax.axis_size("expert")
    dp_count = lax.axis_size("dp")
    chips = dp_count // CORES
    token_rows, model_width = tokens.shape
    top_count = expert_ids.shape[1]
    width = w_gate.shape[1]
    capacity = 2 * token_rows * top_count // EXPERTS
    slot_total = expert_count * capacity
    me_z = lax.axis_index("expert")
    me_d = lax.axis_index("dp")

    def to_dp(array, mask):
        return lax.ppermute(array, "dp", [(i, i ^ mask) for i in range(dp_count)])

    def to_expert(array, step):
        pairs = [(i, (i + step) % expert_count) for i in range(expert_count)]
        return lax.ppermute(array, "expert", pairs)

    own = (w_gate[0], w_up[0], w_down[0])
    pieces = [{0: w} for w in own]
    for mask in range(CORES, dp_count, CORES):
        for k in range(3):
            pieces[k][mask] = to_dp(own[k], mask)
    for mask in range(0, dp_count, CORES):
        for k in range(3):
            pieces[k][mask + 1] = to_dp(pieces[k][mask], 1)
    gate_p, up_p, down_p = pieces

    wanted = (me_z + jnp.arange(expert_count, dtype=jnp.int32)) % expert_count
    hit = expert_ids[:, :, None] == wanted[None, None, :]
    named = jnp.any(hit, axis=1)
    before = jnp.arange(token_rows)[:, None] > jnp.arange(token_rows)[None, :]
    slot = dot(before.astype(jnp.bfloat16), named.astype(jnp.bfloat16))
    chosen = named[:, :, None] & (
        slot[:, :, None] == jnp.arange(capacity, dtype=jnp.float32)[None, None, :]
    )
    select = chosen.reshape(token_rows, slot_total).astype(jnp.bfloat16)
    prob = jnp.sum(jnp.where(hit, gate_probs[:, :, None], 0.0), axis=1)

    def turned(array):
        return jnp.concatenate(
            [
                lax.dynamic_slice_in_dim(array, (me_d ^ j) * width, width, 1)
                for j in range(dp_count)
            ],
            axis=1,
        )

    tokens_t = turned(tokens)
    cot_t = turned(cotangent)
    send_x = dot_first(select, tokens_t).astype(jnp.bfloat16)
    send_dy = dot_first(select, cot_t).astype(jnp.bfloat16)
    send = jnp.concatenate(
        [
            send_x.reshape(expert_count, capacity, model_width),
            send_dy.reshape(expert_count, capacity, model_width),
        ],
        axis=1,
    )
    got = [send[0]] + [to_expert(send[j], j) for j in range(1, expert_count)]
    rows_x = jnp.concatenate([g[:capacity] for g in got], axis=0)
    rows_dy = jnp.concatenate([g[capacity:] for g in got], axis=0)

    def cols(array, j, n=1):
        return array[:, j * width : (j + n) * width]

    gate_part = sum(dot(cols(rows_x, j), gate_p[j]) for j in range(dp_count))
    up_part = sum(dot(cols(rows_x, j), up_p[j]) for j in range(dp_count))
    back_hidden = sum(dot_last(cols(rows_dy, j), down_p[j]) for j in range(dp_count))
    sigmoid_gate = jax.nn.sigmoid(gate_part)
    activated = gate_part * sigmoid_gate
    hidden = (activated * up_part).astype(jnp.bfloat16)
    d_gate = (
        back_hidden * up_part * sigmoid_gate * (1.0 + gate_part * (1.0 - sigmoid_gate))
    ).astype(jnp.bfloat16)
    d_up = (back_hidden * activated).astype(jnp.bfloat16)
    expert_out = jnp.concatenate(
        [dot(hidden, down_p[j]).astype(jnp.bfloat16) for j in range(dp_count)], axis=1
    )
    d_rows = jnp.concatenate(
        [
            (dot_last(d_gate, gate_p[j]) + dot_last(d_up, up_p[j])).astype(jnp.bfloat16)
            for j in range(dp_count)
        ],
        axis=1,
    )
    back = jnp.concatenate(
        [
            expert_out.reshape(expert_count, capacity, model_width),
            d_rows.reshape(expert_count, capacity, model_width),
        ],
        axis=1,
    )
    home = [back[0]] + [to_expert(back[j], -j) for j in range(1, expert_count)]
    back_out = jnp.concatenate([h[:capacity] for h in home], axis=0)
    back_rows = jnp.concatenate([h[capacity:] for h in home], axis=0)

    trio = jnp.concatenate([hidden, d_gate, d_up], axis=1)
    pair = jnp.concatenate([rows_x, rows_dy], axis=0)
    trios, pairs = [trio], [cols(pair, 0, CORES)]
    for mask in range(CORES, dp_count, CORES):
        pairs.append(to_dp(cols(pair, mask, CORES), mask))
        trios.append(to_dp(trio, mask))
    all_trio = jnp.concatenate(trios, axis=0)
    all_x = jnp.concatenate([p[:slot_total] for p in pairs], axis=0)
    all_dy = jnp.concatenate([p[slot_total:] for p in pairs], axis=0)
    ff = w_gate.shape[2]

    def reduced(part_own, part_other):
        return (part_own + to_dp(part_other.astype(jnp.bfloat16), 1).astype(jnp.float32)).astype(
            jnp.bfloat16
        )

    all_h, all_g, all_u = (all_trio[:, k * ff : (k + 1) * ff] for k in range(3))
    grad_w_gate = reduced(dot_first(cols(all_x, 0), all_g), dot_first(cols(all_x, 1), all_g))[None]
    grad_w_up = reduced(dot_first(cols(all_x, 0), all_u), dot_first(cols(all_x, 1), all_u))[None]
    grad_w_down = reduced(dot_first(all_h, cols(all_dy, 0)), dot_first(all_h, cols(all_dy, 1)))[
        None
    ]

    table = jnp.where(chosen, prob[:, :, None], 0.0).reshape(token_rows, slot_total)
    high = table.astype(jnp.bfloat16)
    rest = table - high.astype(jnp.float32)
    middle = rest.astype(jnp.bfloat16)
    low = (rest - middle.astype(jnp.float32)).astype(jnp.bfloat16)

    def weighted(rows):
        total = dot(high, rows) + (dot(middle, rows) + dot(low, rows))
        return turned(total.astype(jnp.bfloat16))

    mixed = weighted(back_out)
    grad_tokens = weighted(back_rows)
    inner = jnp.sum(
        jnp.where(
            chosen, dot_last(cot_t, back_out).reshape(token_rows, expert_count, capacity), 0.0
        ),
        axis=2,
    )
    grad_gates = jnp.sum(jnp.where(hit, inner[:, None, :], 0.0), axis=2)
    return (mixed, grad_tokens, grad_gates, grad_w_gate, grad_w_up, grad_w_down)


def solution(mesh):
    rows = P(("groups", "expert", "dp"), None)
    in_specs = (
        rows,
        rows,
        rows,
        rows,
        P("expert", "dp", None),
        P("expert", "dp", None),
        P("expert", None, "dp"),
    )
    out_specs = (
        rows,
        rows,
        rows,
        P(("groups", "expert"), "dp", None),
        P(("groups", "expert"), "dp", None),
        P(("groups", "expert"), None, "dp"),
    )
    return jax.shard_map(
        on_device, mesh=mesh, in_specs=in_specs, out_specs=out_specs, check_vma=False
    )
```

```python
import jax
import jax.numpy as jnp
from jax import lax
from jax.sharding import PartitionSpec as P

EXPERTS = 128
CORES = 2


def dot_first(left, right):
    return lax.dot_general(
        left, right, (((0,), (0,)), ((), ())), preferred_element_type=jnp.float32
    )


def dot_last(left, right):
    return lax.dot_general(
        left, right, (((1,), (1,)), ((), ())), preferred_element_type=jnp.float32
    )


def dot(left, right):
    return jnp.dot(left, right, preferred_element_type=jnp.float32)


def on_device(tokens, cotangent, expert_ids, gate_probs, w_gate, w_up, w_down):
    expert_count = lax.axis_size("expert")
    dp_count = lax.axis_size("dp")
    token_rows, model_width = tokens.shape
    top_count = expert_ids.shape[1]
    width = w_gate.shape[1]
    capacity = 2 * token_rows * top_count // EXPERTS
    slot_total = expert_count * capacity
    me_z = lax.axis_index("expert")
    me_d = lax.axis_index("dp")

    def to_dp(array, mask):
        return lax.ppermute(array, "dp", [(i, i ^ mask) for i in range(dp_count)])

    even = expert_count & (expert_count - 1) == 0

    def to_expert(array, step):
        if even:
            pairs = [(i, i ^ step) for i in range(expert_count)]
        else:
            pairs = [(i, (i + step) % expert_count) for i in range(expert_count)]
        return lax.ppermute(array, "expert", pairs)

    def after(values, *others):
        return lax.optimization_barrier((values, others))[0]

    own = (w_gate[0], w_up[0], w_down[0])
    paired = lax.axis_size("groups") == 2
    first_group = lax.axis_index("groups") == 0

    def to_group(array):
        return lax.ppermute(array, "groups", [(0, 1), (1, 0)])

    def near_far(first, second):
        return (first, second) if not paired else pick(first_group, first, second)

    def pick(flag, first, second):
        return (jnp.where(flag, first, second), jnp.where(flag, second, first))

    lead = near_far(own[0], own[1])[0]
    masks = range(CORES, dp_count, CORES)
    lead_got = {mask: to_dp(lead, mask) for mask in masks}
    down_got = {mask: to_dp(own[2], mask) for mask in masks}
    other_got = {
        mask: to_group(lead_got[mask]) if paired else to_dp(own[1], mask) for mask in masks
    }
    pieces = {0: own, 1: tuple(to_dp(w, 1) for w in own)}

    steps = jnp.arange(expert_count, dtype=jnp.int32)
    wanted = me_z ^ steps if even else (me_z + steps) % expert_count
    hit = expert_ids[:, :, None] == wanted[None, None, :]
    named = jnp.any(hit, axis=1)
    before = jnp.arange(token_rows)[:, None] > jnp.arange(token_rows)[None, :]
    slot = dot(before.astype(jnp.bfloat16), named.astype(jnp.bfloat16))
    chosen = named[:, :, None] & (
        slot[:, :, None] == jnp.arange(capacity, dtype=jnp.float32)[None, None, :]
    )
    select = chosen.reshape(token_rows, slot_total).astype(jnp.bfloat16)
    prob = jnp.sum(jnp.where(hit, gate_probs[:, :, None], 0.0), axis=1)

    def turned(array):
        return jnp.concatenate(
            [
                lax.dynamic_slice_in_dim(array, (me_d ^ j) * width, width, 1)
                for j in range(dp_count)
            ],
            axis=1,
        )

    tokens_t = turned(tokens)
    cot_t = turned(cotangent)
    send_x = dot_first(select, tokens_t).astype(jnp.bfloat16)
    send_dy = dot_first(select, cot_t).astype(jnp.bfloat16)
    send = jnp.concatenate(
        [
            send_x.reshape(expert_count, capacity, model_width),
            send_dy.reshape(expert_count, capacity, model_width),
        ],
        axis=1,
    )
    order = [1, *range(expert_count - 1, 1, -1)]
    send = after(send, pieces[1])
    got = [send[0]] + [None] * (expert_count - 1)
    for j in order:
        got[j] = to_expert(send[j], j)
    for mask in masks:
        pieces[mask] = (lead_got[mask], other_got[mask], down_got[mask])
        sibling = [to_dp(after(w, got), 1) for w in (lead_got[mask], down_got[mask])]
        pieces[mask + 1] = (sibling[0], to_dp(other_got[mask], 1), sibling[1])
    rows_x = jnp.concatenate([g[:capacity] for g in got], axis=0)
    rows_dy = jnp.concatenate([g[capacity:] for g in got], axis=0)

    def cols(array, j, n=1):
        return array[:, j * width : (j + n) * width]

    local = range(CORES)
    remote = range(CORES, dp_count)

    def side(rows, k, js):
        return sum(dot(cols(rows, j), pieces[j][k]) for j in js)

    far = near_far(side(rows_x, 0, remote), side(rows_x, 1, remote))
    gate_part = side(rows_x, 0, local) + far[0]
    up_part = side(rows_x, 1, local) + far[1]
    back_hidden = sum(dot_last(cols(rows_dy, j), pieces[j][2]) for j in range(dp_count))
    sigmoid_gate = jax.nn.sigmoid(gate_part)
    activated = gate_part * sigmoid_gate
    hidden = (activated * up_part).astype(jnp.bfloat16)
    d_gate = (
        back_hidden * up_part * sigmoid_gate * (1.0 + gate_part * (1.0 - sigmoid_gate))
    ).astype(jnp.bfloat16)
    d_up = (back_hidden * activated).astype(jnp.bfloat16)
    expert_out = jnp.concatenate(
        [dot(hidden, pieces[j][2]).astype(jnp.bfloat16) for j in range(dp_count)], axis=1
    )
    d_pair = {j: (d_gate, d_up) if j < CORES else near_far(d_gate, d_up) for j in range(dp_count)}
    d_rows = jnp.concatenate(
        [
            (dot_last(d_pair[j][0], pieces[j][0]) + dot_last(d_pair[j][1], pieces[j][1])).astype(
                jnp.bfloat16
            )
            for j in range(dp_count)
        ],
        axis=1,
    )
    back = jnp.concatenate(
        [
            expert_out.reshape(expert_count, capacity, model_width),
            d_rows.reshape(expert_count, capacity, model_width),
        ],
        axis=1,
    )
    home = [back[0]] + [None] * (expert_count - 1)
    for j in order:
        home[j] = to_expert(back[j], j if even else -j)

    trio = jnp.concatenate([hidden, d_gate, d_up], axis=1)
    pair = jnp.concatenate([rows_x, rows_dy], axis=0)
    pair_far = after(pair, pieces[dp_count - 1])
    trios, pairs = [trio], [cols(pair, 0, CORES)]
    for mask in range(CORES, dp_count, CORES):
        pairs.append(to_dp(cols(pair_far, mask, CORES), mask))
        trios.append(to_dp(trio, mask))
    trios, pairs = after((trios, pairs), home[order[0]])
    all_trio = jnp.concatenate(trios, axis=0)
    all_x = jnp.concatenate([p[:slot_total] for p in pairs], axis=0)
    all_dy = jnp.concatenate([p[slot_total:] for p in pairs], axis=0)
    ff = w_gate.shape[2]

    all_h, all_gu = all_trio[:, :ff], all_trio[:, ff:]

    def reduced(half):
        mine, theirs = half(0), half(1)
        return (mine + to_dp(theirs.astype(jnp.bfloat16), 1).astype(jnp.float32)).astype(
            jnp.bfloat16
        )

    grad_gu = reduced(lambda c: dot_first(cols(all_x, c), all_gu))
    grad_down = reduced(lambda c: dot_first(all_h, cols(all_dy, c)))
    home, grad_gu, grad_down = lax.optimization_barrier((home, grad_gu, grad_down))
    grad_w_gate, grad_w_up, grad_w_down = grad_gu[None, :, :ff], grad_gu[None, :, ff:], grad_down[None]

    back_out = jnp.concatenate([h[:capacity] for h in home], axis=0)
    back_rows = jnp.concatenate([h[capacity:] for h in home], axis=0)
    table = jnp.where(chosen, prob[:, :, None], 0.0).reshape(token_rows, slot_total)
    high = table.astype(jnp.bfloat16)
    rest = table - high.astype(jnp.float32)
    middle = rest.astype(jnp.bfloat16)
    low = (rest - middle.astype(jnp.float32)).astype(jnp.bfloat16)

    def weighted(rows):
        total = dot(high, rows) + (dot(middle, rows) + dot(low, rows))
        return turned(total.astype(jnp.bfloat16))

    mixed = weighted(back_out)
    grad_tokens = weighted(back_rows)
    inner = jnp.sum(
        jnp.where(
            chosen, dot_last(cot_t, back_out).reshape(token_rows, expert_count, capacity), 0.0
        ),
        axis=2,
    )
    grad_gates = jnp.sum(jnp.where(hit, inner[:, None, :], 0.0), axis=2)
    return (mixed, grad_tokens, grad_gates, grad_w_gate, grad_w_up, grad_w_down)


def solution(mesh):
    rows = P(("groups", "expert", "dp"), None)
    in_specs = (
        rows,
        rows,
        rows,
        rows,
        P("expert", "dp", None),
        P("expert", "dp", None),
        P("expert", None, "dp"),
    )
    out_specs = (
        rows,
        rows,
        rows,
        P(("groups", "expert"), "dp", None),
        P(("groups", "expert"), "dp", None),
        P(("groups", "expert"), None, "dp"),
    )
    return jax.shard_map(
        on_device, mesh=mesh, in_specs=in_specs, out_specs=out_specs, check_vma=False
    )
```

```python
import jax
import jax.numpy as jnp
from jax import lax
from jax.experimental import pallas as pl
from jax.experimental.pallas import tpu as pltpu
from jax.sharding import PartitionSpec as P

EXPERTS = 128
CORES = 2


def dot_first(left, right):
    return lax.dot_general(
        left, right, (((0,), (0,)), ((), ())), preferred_element_type=jnp.float32
    )


def dot_last(left, right):
    return lax.dot_general(
        left, right, (((1,), (1,)), ((), ())), preferred_element_type=jnp.float32
    )


def dot(left, right):
    return jnp.dot(left, right, preferred_element_type=jnp.float32)


def choose_kernel(flag_ref, first_ref, second_ref, out_ref, sem):
    @pl.when(flag_ref[0] == 0)
    def _():
        copy = pltpu.make_async_copy(first_ref, out_ref, sem)
        copy.start()
        copy.wait()

    @pl.when(flag_ref[0] != 0)
    def _():
        copy = pltpu.make_async_copy(second_ref, out_ref, sem)
        copy.start()
        copy.wait()


def choose(flag, first, second):
    anywhere = pl.BlockSpec(memory_space=pl.ANY)
    return pl.pallas_call(
        choose_kernel,
        out_shape=jax.ShapeDtypeStruct(first.shape, first.dtype),
        in_specs=[pl.BlockSpec(memory_space=pltpu.SMEM), anywhere, anywhere],
        out_specs=anywhere,
        scratch_shapes=[pltpu.SemaphoreType.DMA],
    )(flag.reshape(1), first, second)


def on_device(tokens, cotangent, expert_ids, gate_probs, w_gate, w_up, w_down):
    expert_count = lax.axis_size("expert")
    dp_count = lax.axis_size("dp")
    token_rows, model_width = tokens.shape
    top_count = expert_ids.shape[1]
    width = w_gate.shape[1]
    capacity = 2 * token_rows * top_count // EXPERTS
    slot_total = expert_count * capacity
    me_z = lax.axis_index("expert")
    me_d = lax.axis_index("dp")

    def to_dp(array, mask):
        return lax.ppermute(array, "dp", [(i, i ^ mask) for i in range(dp_count)])

    even = expert_count & (expert_count - 1) == 0

    def to_expert(array, step):
        if even:
            pairs = [(i, i ^ step) for i in range(expert_count)]
        else:
            pairs = [(i, (i + step) % expert_count) for i in range(expert_count)]
        return lax.ppermute(array, "expert", pairs)

    def after(values, *others):
        return lax.optimization_barrier((values, others))[0]

    own = (w_gate[0], w_up[0], w_down[0])
    paired = lax.axis_size("groups") == 2
    first_group = lax.axis_index("groups") == 0

    def to_group(array):
        return lax.ppermute(array, "groups", [(0, 1), (1, 0)])

    def near_far(first, second):
        return (first, second) if not paired else pick(first_group, first, second)

    def pick(flag, first, second):
        return (jnp.where(flag, first, second), jnp.where(flag, second, first))

    lead = choose(lax.axis_index("groups"), own[0], own[1]) if paired else own[0]
    own = after(own, lead)
    masks = range(CORES, dp_count, CORES)
    lead_got = {mask: to_dp(lead, mask) for mask in masks}
    down_got = {mask: to_dp(own[2], mask) for mask in masks}
    other_got = {
        mask: to_group(lead_got[mask]) if paired else to_dp(own[1], mask) for mask in masks
    }
    pieces = {0: own, 1: tuple(to_dp(w, 1) for w in own)}

    steps = jnp.arange(expert_count, dtype=jnp.int32)
    wanted = me_z ^ steps if even else (me_z + steps) % expert_count
    hit = expert_ids[:, :, None] == wanted[None, None, :]
    named = jnp.any(hit, axis=1)
    before = jnp.arange(token_rows)[:, None] > jnp.arange(token_rows)[None, :]
    slot = dot(before.astype(jnp.bfloat16), named.astype(jnp.bfloat16))
    chosen = named[:, :, None] & (
        slot[:, :, None] == jnp.arange(capacity, dtype=jnp.float32)[None, None, :]
    )
    select = chosen.reshape(token_rows, slot_total).astype(jnp.bfloat16)
    prob = jnp.sum(jnp.where(hit, gate_probs[:, :, None], 0.0), axis=1)

    def turned(array):
        return jnp.concatenate(
            [
                lax.dynamic_slice_in_dim(array, (me_d ^ j) * width, width, 1)
                for j in range(dp_count)
            ],
            axis=1,
        )

    tokens_t = turned(tokens)
    cot_t = turned(cotangent)
    send_x = dot_first(select, tokens_t).astype(jnp.bfloat16)
    send_dy = dot_first(select, cot_t).astype(jnp.bfloat16)
    send = jnp.concatenate(
        [
            send_x.reshape(expert_count, capacity, model_width),
            send_dy.reshape(expert_count, capacity, model_width),
        ],
        axis=1,
    )
    order = [1, *range(expert_count - 1, 1, -1)]
    send = after(send, pieces[1])
    got = [send[0]] + [None] * (expert_count - 1)
    for j in order:
        got[j] = to_expert(send[j], j)
    for mask in masks:
        pieces[mask] = (lead_got[mask], other_got[mask], down_got[mask])
        sibling = [to_dp(after(w, got), 1) for w in (lead_got[mask], down_got[mask])]
        pieces[mask + 1] = (sibling[0], to_dp(other_got[mask], 1), sibling[1])
    rows_x = jnp.concatenate([g[:capacity] for g in got], axis=0)
    rows_dy = jnp.concatenate([g[capacity:] for g in got], axis=0)

    def cols(array, j, n=1):
        return array[:, j * width : (j + n) * width]

    local = range(CORES)
    remote = range(CORES, dp_count)

    def side(rows, k, js):
        return sum(dot(cols(rows, j), pieces[j][k]) for j in js)

    far = near_far(side(rows_x, 0, remote), side(rows_x, 1, remote))
    gate_part = side(rows_x, 0, local) + far[0]
    up_part = side(rows_x, 1, local) + far[1]
    back_hidden = sum(dot_last(cols(rows_dy, j), pieces[j][2]) for j in range(dp_count))
    sigmoid_gate = jax.nn.sigmoid(gate_part)
    activated = gate_part * sigmoid_gate
    hidden = (activated * up_part).astype(jnp.bfloat16)
    d_gate = (
        back_hidden * up_part * sigmoid_gate * (1.0 + gate_part * (1.0 - sigmoid_gate))
    ).astype(jnp.bfloat16)
    d_up = (back_hidden * activated).astype(jnp.bfloat16)
    expert_out = jnp.concatenate(
        [dot(hidden, pieces[j][2]).astype(jnp.bfloat16) for j in range(dp_count)], axis=1
    )
    d_pair = {j: (d_gate, d_up) if j < CORES else near_far(d_gate, d_up) for j in range(dp_count)}
    d_rows = jnp.concatenate(
        [
            (dot_last(d_pair[j][0], pieces[j][0]) + dot_last(d_pair[j][1], pieces[j][1])).astype(
                jnp.bfloat16
            )
            for j in range(dp_count)
        ],
        axis=1,
    )
    back = jnp.concatenate(
        [
            expert_out.reshape(expert_count, capacity, model_width),
            d_rows.reshape(expert_count, capacity, model_width),
        ],
        axis=1,
    )
    home = [back[0]] + [None] * (expert_count - 1)
    for j in order:
        home[j] = to_expert(back[j], j if even else -j)

    trio = jnp.concatenate([hidden, d_gate, d_up], axis=1)
    pair = jnp.concatenate([rows_x, rows_dy], axis=0)
    pair_far = after(pair, pieces[dp_count - 1])
    trios, pairs = [trio], [cols(pair, 0, CORES)]
    for mask in range(CORES, dp_count, CORES):
        pairs.append(to_dp(cols(pair_far, mask, CORES), mask))
        trios.append(to_dp(trio, mask))
    home, trios, pairs = lax.optimization_barrier((home, trios, pairs))
    all_trio = jnp.concatenate(trios, axis=0)
    all_x = jnp.concatenate([p[:slot_total] for p in pairs], axis=0)
    all_dy = jnp.concatenate([p[slot_total:] for p in pairs], axis=0)
    ff = w_gate.shape[2]

    all_h, all_gu = all_trio[:, :ff], all_trio[:, ff:]

    def reduced(half):
        mine, theirs = half(0), half(1)
        return (mine + to_dp(theirs.astype(jnp.bfloat16), 1).astype(jnp.float32)).astype(
            jnp.bfloat16
        )

    grad_gu = reduced(lambda c: dot_first(cols(all_x, c), all_gu))
    grad_down = reduced(lambda c: dot_first(all_h, cols(all_dy, c)))
    grad_w_gate, grad_w_up, grad_w_down = grad_gu[None, :, :ff], grad_gu[None, :, ff:], grad_down[None]

    back_out = jnp.concatenate([h[:capacity] for h in home], axis=0)
    back_rows = jnp.concatenate([h[capacity:] for h in home], axis=0)
    table = jnp.where(chosen, prob[:, :, None], 0.0).reshape(token_rows, slot_total)
    high = table.astype(jnp.bfloat16)
    rest = table - high.astype(jnp.float32)
    middle = rest.astype(jnp.bfloat16)
    low = (rest - middle.astype(jnp.float32)).astype(jnp.bfloat16)

    def weighted(rows):
        total = dot(high, rows) + (dot(middle, rows) + dot(low, rows))
        return turned(total.astype(jnp.bfloat16))

    mixed = weighted(back_out)
    grad_tokens = weighted(back_rows)
    inner = jnp.sum(
        jnp.where(
            chosen, dot_last(cot_t, back_out).reshape(token_rows, expert_count, capacity), 0.0
        ),
        axis=2,
    )
    grad_gates = jnp.sum(jnp.where(hit, inner[:, None, :], 0.0), axis=2)
    return (mixed, grad_tokens, grad_gates, grad_w_gate, grad_w_up, grad_w_down)


def solution(mesh):
    rows = P(("groups", "expert", "dp"), None)
    in_specs = (
        rows,
        rows,
        rows,
        rows,
        P("expert", "dp", None),
        P("expert", "dp", None),
        P("expert", None, "dp"),
    )
    out_specs = (
        rows,
        rows,
        rows,
        P(("groups", "expert"), "dp", None),
        P(("groups", "expert"), "dp", None),
        P(("groups", "expert"), None, "dp"),
    )
    return jax.shard_map(
        on_device, mesh=mesh, in_specs=in_specs, out_specs=out_specs, check_vma=False
    )
```

```python
import jax
import jax.numpy as jnp
from jax import lax
from jax.experimental import pallas as pl
from jax.experimental.pallas import tpu as pltpu
from jax.sharding import PartitionSpec as P

EXPERTS = 128
CORES = 2
BF16 = jnp.bfloat16
F32 = jnp.float32
VMEM_LIMIT = 16 << 20


def dot(left, right):
    return jnp.dot(left, right, preferred_element_type=F32)


def dot_first(left, right):
    return lax.dot_general(left, right, (((0,), (0,)), ((), ())), preferred_element_type=F32)


def dot_last(left, right):
    return lax.dot_general(left, right, (((1,), (1,)), ((), ())), preferred_element_type=F32)


def shape(dims, dtype=BF16):
    return jax.ShapeDtypeStruct(dims, dtype)


def call(kernel, out_shape, *args, smem=0, scratch=(), flops=0, anywhere=()):
    vmem = pl.BlockSpec(memory_space=pltpu.VMEM)
    specs = [
        pl.BlockSpec(memory_space=pltpu.SMEM)
        if i < smem
        else pl.BlockSpec(memory_space=pl.ANY)
        if i in anywhere
        else vmem
        for i in range(len(args))
    ]
    return pl.pallas_call(
        kernel,
        out_shape=out_shape,
        in_specs=specs,
        out_specs=jax.tree.map(lambda _: vmem, out_shape),
        scratch_shapes=list(scratch),
        compiler_params=pltpu.CompilerParams(vmem_limit_bytes=VMEM_LIMIT),
        cost_estimate=pl.CostEstimate(flops=flops, bytes_accessed=1, transcendentals=0),
    )(*args)


def choose(flag, first, second):
    def kernel(flag_ref, first_ref, second_ref, out_ref, sem):
        @pl.when(flag_ref[0] == 0)
        def _():
            copy = pltpu.make_async_copy(first_ref, out_ref, sem)
            copy.start()
            copy.wait()

        @pl.when(flag_ref[0] != 0)
        def _():
            copy = pltpu.make_async_copy(second_ref, out_ref, sem)
            copy.start()
            copy.wait()

    return call(
        kernel,
        shape(first.shape),
        flag.reshape(1),
        first,
        second,
        smem=1,
        anywhere=(1, 2),
        scratch=[pltpu.SemaphoreType.DMA],
    )


def slots(place, ids, probs, tokens, cotangent, expert_count, capacity, dp_count, even):
    top_count, token_rows = ids.shape
    width = tokens.shape[1] // dp_count
    total = expert_count * capacity

    def kernel(place_ref, ids_ref, probs_ref, x_ref, dy_ref, *outs):
        chunks, (select_ref, table_ref) = outs[:expert_count], outs[expert_count:]
        row = lax.broadcasted_iota(jnp.int32, (total, token_rows), 0)
        step = row // capacity
        far = step + place_ref[0]
        wanted = step ^ place_ref[0] if even else jnp.where(far >= expert_count, far - expert_count, far)
        named = jnp.zeros((total, token_rows), F32)
        prob = jnp.zeros((total, token_rows), F32)
        for k in range(top_count):
            hit = ids_ref[k : k + 1, :] == wanted
            named = jnp.where(hit, 1.0, named)
            prob = jnp.where(hit, probs_ref[k : k + 1, :], prob)
        earlier = lax.broadcasted_iota(jnp.int32, (token_rows, token_rows), 0)
        later = lax.broadcasted_iota(jnp.int32, (token_rows, token_rows), 1)
        before = jnp.where(earlier < later, 1.0, 0.0).astype(BF16)
        slot = dot(named.astype(BF16), before)
        own_slot = (row - step * capacity).astype(F32)
        select = jnp.where((named > 0.5) & (slot == own_slot), 1.0, 0.0)
        pick = select.astype(BF16)
        select_ref[...] = pick
        for j in range(dp_count):
            source = pl.ds(pl.multiple_of((place_ref[1] ^ j) * width, width), width)
            target = slice(j * width, (j + 1) * width)
            rows_x = dot(pick, x_ref[:, source]).astype(BF16)
            rows_dy = dot(pick, dy_ref[:, source]).astype(BF16)
            for e in range(expert_count):
                part = slice(e * capacity, (e + 1) * capacity)
                chunks[e][0:capacity, target] = rows_x[part]
                chunks[e][capacity:, target] = rows_dy[part]
        table = (select * prob).T
        high = table.astype(BF16)
        rest = table - high.astype(F32)
        middle = rest.astype(BF16)
        table_ref[:, 0:total] = high
        table_ref[:, total : 2 * total] = middle
        table_ref[:, 2 * total :] = (rest - middle.astype(F32)).astype(BF16)

    outs = [shape((2 * capacity, tokens.shape[1]))] * expert_count
    outs += [shape((total, token_rows)), shape((token_rows, 3 * total))]
    got = call(kernel, outs, place, ids, probs, tokens, cotangent, smem=1)
    return got[:expert_count], got[expert_count], got[expert_count + 1]


def first_half(chunks, pieces, near, width):
    count, dp_count = len(chunks), len(pieces)
    capacity = chunks[0].shape[0] // 2
    total = count * capacity
    model_width = chunks[0].shape[1]
    ff = pieces[0][2].shape[0]
    weights = [w for p in pieces for w in p if w is not None]

    def kernel(*refs):
        chunk_refs, refs = refs[:count], refs[count:]
        weight_refs, (rows_ref, keep_ref, send_ref, sums_ref) = refs[: len(weights)], refs[len(weights) :]
        for e in range(count):
            rows_ref[e * capacity : (e + 1) * capacity, :] = chunk_refs[e][0:capacity, :]
            rows_ref[total + e * capacity : total + (e + 1) * capacity, :] = chunk_refs[e][capacity:, :]
        keep_ref[...] = rows_ref[:, 0 : near * width]
        send_ref[...] = rows_ref[:, near * width :]
        sums = [0.0, 0.0, 0.0, 0.0]
        at = 0
        for j, piece in enumerate(pieces):
            column = slice(j * width, (j + 1) * width)
            x, dy = rows_ref[0:total, column], rows_ref[total:, column]
            if j < near:
                sums[0] += dot(x, weight_refs[at][...])
                sums[1] += dot(x, weight_refs[at + 1][...])
                sums[3] += dot_last(dy, weight_refs[at + 2][...])
                at += 3
            else:
                sums[2] += dot(x, weight_refs[at][...])
                sums[3] += dot_last(dy, weight_refs[at + 1][...])
                at += 2
        for k in range(4):
            sums_ref[:, k * ff : (k + 1) * ff] = sums[k]

    outs = [
        shape((2 * total, model_width)),
        shape((2 * total, near * width)),
        shape((2 * total, model_width - near * width)),
        shape((total, 4 * ff), F32),
    ]
    return call(kernel, outs, *chunks, *weights)


def second_half(flag, rows, sums, pieces, near, width, count):
    total = rows.shape[0] // 2
    capacity = total // count
    model_width = rows.shape[1]
    ff = sums.shape[1] // 4
    weights = [w for p in pieces for w in p]
    far = [j for j in range(len(pieces)) if j >= near]

    def kernel(flag_ref, rows_ref, sums_ref, *refs):
        weight_refs, outs = refs[: len(weights)], refs[len(weights) :]
        chunk_refs, trio_ref = outs[:count], outs[count]
        last = 0.0
        for j in far:
            last += dot(rows_ref[0:total, j * width : (j + 1) * width], weight_refs[3 * j + 1][...])
        lead = sums_ref[:, 2 * ff : 3 * ff]
        swapped = flag_ref[0] != 0
        gate_part = sums_ref[:, 0:ff] + jnp.where(swapped, last, lead)
        up_part = sums_ref[:, ff : 2 * ff] + jnp.where(swapped, lead, last)
        back_hidden = sums_ref[:, 3 * ff :]
        sigmoid_gate = jax.nn.sigmoid(gate_part)
        activated = gate_part * sigmoid_gate
        hidden = (activated * up_part).astype(BF16)
        d_gate = back_hidden * up_part * sigmoid_gate * (1.0 + gate_part * (1.0 - sigmoid_gate))
        d_up = back_hidden * activated
        far_first = jnp.where(swapped, d_up, d_gate).astype(BF16)
        far_second = jnp.where(swapped, d_gate, d_up).astype(BF16)
        d_gate, d_up = d_gate.astype(BF16), d_up.astype(BF16)
        trio_ref[:, 0:ff] = hidden
        trio_ref[:, ff : 2 * ff] = d_gate
        trio_ref[:, 2 * ff :] = d_up
        for j in range(len(pieces)):
            column = slice(j * width, (j + 1) * width)
            one, two = (d_gate, d_up) if j < near else (far_first, far_second)
            out = dot(hidden, weight_refs[3 * j + 2][...]).astype(BF16)
            back = dot_last(one, weight_refs[3 * j][...]) + dot_last(two, weight_refs[3 * j + 1][...])
            back = back.astype(BF16)
            for e in range(count):
                part = slice(e * capacity, (e + 1) * capacity)
                chunk_refs[e][0:capacity, column] = out[part]
                chunk_refs[e][capacity:, column] = back[part]

    outs = [shape((2 * capacity, model_width))] * count + [shape((total, 3 * ff))]
    got = call(kernel, outs, flag, rows, sums, *weights, smem=1)
    return got[:count], got[count]


def gradients(keeps, trios, width, ff):
    count = len(keeps)

    def kernel(*refs):
        keep_refs, trio_refs = refs[:count], refs[count : 2 * count]
        gate_ref, up_ref, down_ref = refs[2 * count :]
        half = keep_refs[0].shape[0] // 2
        x = jnp.concatenate([r[0:half, 0:width] for r in keep_refs], axis=0)
        dy = jnp.concatenate([r[half:, 0:width] for r in keep_refs], axis=0)
        trio = jnp.concatenate([r[...] for r in trio_refs], axis=0)
        gate_ref[...] = dot_first(x, trio[:, ff : 2 * ff]).astype(BF16)
        up_ref[...] = dot_first(x, trio[:, 2 * ff :]).astype(BF16)
        down_ref[...] = dot_first(trio[:, 0:ff], dy).astype(BF16)

    outs = [shape((width, ff)), shape((width, ff)), shape((ff, width))]
    return call(kernel, outs, *keeps, *trios)


def collect(place, ids, select, table, cotangent, chunks, dp_count, even):
    count = len(chunks)
    capacity = chunks[0].shape[0] // 2
    total = count * capacity
    token_rows, model_width = cotangent.shape
    width = model_width // dp_count

    def kernel(place_ref, ids_ref, select_ref, table_ref, dy_ref, *refs):
        chunk_refs, (mixed_ref, grad_ref, gates_ref) = refs[:count], refs[count:]
        inner = 0.0
        for j in range(dp_count):
            column = slice(j * width, (j + 1) * width)
            home = pl.ds(pl.multiple_of((place_ref[1] ^ j) * width, width), width)
            out = jnp.concatenate([r[0:capacity, column] for r in chunk_refs], axis=0)
            back = jnp.concatenate([r[capacity:, column] for r in chunk_refs], axis=0)
            mixed_ref[:, home] = dot(table_ref[...], jnp.concatenate([out] * 3, axis=0)).astype(BF16)
            grad_ref[:, home] = dot(table_ref[...], jnp.concatenate([back] * 3, axis=0)).astype(BF16)
            inner += dot_last(out, dy_ref[:, home])
        inner = jnp.where(select_ref[...] > 0, inner, 0.0)
        step = lax.broadcasted_iota(jnp.int32, (total, token_rows), 0) // capacity
        far = step + place_ref[0]
        wanted = step ^ place_ref[0] if even else jnp.where(far >= count, far - count, far)
        for k in range(ids_ref.shape[0]):
            hit = ids_ref[k : k + 1, :] == wanted
            gates_ref[k : k + 1, :] = jnp.sum(jnp.where(hit, inner, 0.0), axis=0, keepdims=True)

    outs = [
        shape((token_rows, model_width)),
        shape((token_rows, model_width)),
        shape(ids.shape, F32),
    ]
    return call(kernel, outs, place, ids, select, table, cotangent, *chunks, smem=1)


def on_device(tokens, cotangent, expert_ids, gate_probs, w_gate, w_up, w_down):
    expert_count = lax.axis_size("expert")
    dp_count = lax.axis_size("dp")
    token_rows = tokens.shape[0]
    width, ff = w_gate.shape[1:]
    capacity = 2 * token_rows * expert_ids.shape[1] // EXPERTS
    group = lax.axis_index("groups").astype(jnp.int32)
    place = jnp.stack([lax.axis_index("expert"), lax.axis_index("dp")]).astype(jnp.int32)
    even = expert_count & (expert_count - 1) == 0
    paired = lax.axis_size("groups") == 2
    flag = (group if paired else jnp.zeros_like(group)).reshape(1)

    def to_dp(array, mask):
        return lax.ppermute(array, "dp", [(i, i ^ mask) for i in range(dp_count)])

    def to_group(array):
        return lax.ppermute(array, "groups", [(0, 1), (1, 0)])

    def to_expert(array, step):
        if even:
            pairs = [(i, i ^ step) for i in range(expert_count)]
        else:
            pairs = [(i, (i + step) % expert_count) for i in range(expert_count)]
        return lax.ppermute(array, "expert", pairs)

    def after(values, *others):
        return lax.optimization_barrier((values, others))[0]

    own = (w_gate[0], w_up[0], w_down[0])
    lead = choose(group, own[0], own[1]) if paired else own[0]
    own = after(own, lead)
    masks = range(CORES, dp_count, CORES)
    lead_got = {mask: to_dp(lead, mask) for mask in masks}
    other_got = {
        mask: to_group(lead_got[mask]) if paired else to_dp(own[1], mask) for mask in masks
    }
    sibling = tuple(to_dp(w, 1) for w in own)

    ids, probs = expert_ids.T, gate_probs.T
    send, select, table = slots(
        place, ids, probs, tokens, cotangent, expert_count, capacity, dp_count, even
    )
    order = [1, *range(expert_count - 1, 1, -1)]
    send = after(send, sibling)
    down = after(own[2], send)
    down_got = {mask: to_dp(down, mask) for mask in masks}
    got = [send[0]] + [None] * (expert_count - 1)
    for j in order:
        got[j] = to_expert(send[j], j)

    early = [(own[0], own[1], own[2]), (sibling[0], sibling[1], sibling[2])]
    full = list(early)
    for mask in masks:
        lead_sib, down_sib = (to_dp(after(w, got), 1) for w in (lead_got[mask], down_got[mask]))
        early += [(lead_got[mask], None, down_got[mask]), (lead_sib, None, down_sib)]
        other_sib = to_dp(other_got[mask], 1)
        full += [
            (lead_got[mask], other_got[mask], down_got[mask]),
            (lead_sib, other_sib, down_sib),
        ]
    rows, keep, far_rows, sums = first_half(got, early, CORES, width)
    back, trio = second_half(flag, rows, sums, full, CORES, width, expert_count)

    home = [back[0]] + [None] * (expert_count - 1)
    for j in order:
        home[j] = to_expert(back[j], j if even else -j)

    kept = [keep]
    for i, mask in enumerate(masks):
        part = far_rows[:, i * CORES * width : (i + 1) * CORES * width]
        kept.append(to_dp(part, mask))
    trios = [trio] + [to_dp(trio, mask) for mask in masks]
    trios, kept = lax.optimization_barrier((trios, kept))
    theirs = to_dp(jnp.concatenate([k[:, width:] for k in kept], axis=0), 1)
    size = keep.shape[0]
    kept += [theirs[i * size : (i + 1) * size] for i in range(len(kept))]
    trios += [to_dp(t, 1) for t in trios]

    home, kept, trios = lax.optimization_barrier((home, kept, trios))
    mixed, grad_tokens, grad_gates = collect(
        place, ids, select, table, cotangent, home, dp_count, even
    )
    grad_w_gate, grad_w_up, grad_w_down = gradients(kept, trios, width, ff)
    return (
        mixed,
        grad_tokens,
        grad_gates.T,
        grad_w_gate[None],
        grad_w_up[None],
        grad_w_down[None],
    )


def solution(mesh):
    rows = P(("groups", "expert", "dp"), None)
    in_specs = (
        rows,
        rows,
        rows,
        rows,
        P("expert", "dp", None),
        P("expert", "dp", None),
        P("expert", None, "dp"),
    )
    out_specs = (
        rows,
        rows,
        rows,
        P(("groups", "expert"), "dp", None),
        P(("groups", "expert"), "dp", None),
        P(("groups", "expert"), None, "dp"),
    )
    return jax.shard_map(
        on_device, mesh=mesh, in_specs=in_specs, out_specs=out_specs, check_vma=False
    )
```

```python
import jax
import jax.numpy as jnp
from jax import lax
from jax.experimental import pallas as pl
from jax.experimental.pallas import tpu as pltpu
from jax.sharding import PartitionSpec as P

EXPERTS = 128
CORES = 2
BF16 = jnp.bfloat16
F32 = jnp.float32
VMEM_LIMIT = 16 << 20
FIRST_WEIGHT = 1 << 36
COLLECT_WEIGHT = 1 << 33


def dot(left, right):
    return jnp.dot(left, right, preferred_element_type=F32)


def dot_first(left, right):
    return lax.dot_general(left, right, (((0,), (0,)), ((), ())), preferred_element_type=F32)


def dot_last(left, right):
    return lax.dot_general(left, right, (((1,), (1,)), ((), ())), preferred_element_type=F32)


def shape(dims, dtype=BF16):
    return jax.ShapeDtypeStruct(dims, dtype)


def call(kernel, out_shape, *args, smem=0, scratch=(), flops=0, anywhere=(), weight=1):
    vmem = pl.BlockSpec(memory_space=pltpu.VMEM)
    specs = [
        pl.BlockSpec(memory_space=pltpu.SMEM)
        if i < smem
        else pl.BlockSpec(memory_space=pl.ANY)
        if i in anywhere
        else vmem
        for i in range(len(args))
    ]
    return pl.pallas_call(
        kernel,
        out_shape=out_shape,
        in_specs=specs,
        out_specs=jax.tree.map(lambda _: vmem, out_shape),
        scratch_shapes=list(scratch),
        compiler_params=pltpu.CompilerParams(vmem_limit_bytes=VMEM_LIMIT),
        cost_estimate=pl.CostEstimate(flops=weight, bytes_accessed=1, transcendentals=0),
    )(*args)


def choose(flag, first, second):
    def kernel(flag_ref, first_ref, second_ref, out_ref, sem):
        @pl.when(flag_ref[0] == 0)
        def _():
            copy = pltpu.make_async_copy(first_ref, out_ref, sem)
            copy.start()
            copy.wait()

        @pl.when(flag_ref[0] != 0)
        def _():
            copy = pltpu.make_async_copy(second_ref, out_ref, sem)
            copy.start()
            copy.wait()

    return call(
        kernel,
        shape(first.shape),
        flag.reshape(1),
        first,
        second,
        smem=1,
        anywhere=(1, 2),
        scratch=[pltpu.SemaphoreType.DMA],
    )


def slots(place, ids, probs, tokens, cotangent, expert_count, capacity, dp_count, even):
    top_count, token_rows = ids.shape
    width = tokens.shape[1] // dp_count
    total = expert_count * capacity

    def kernel(place_ref, ids_ref, probs_ref, x_ref, dy_ref, *outs):
        chunks, (select_ref, table_ref) = outs[:expert_count], outs[expert_count:]
        row = lax.broadcasted_iota(jnp.int32, (total, token_rows), 0)
        step = row // capacity
        far = step + place_ref[0]
        wanted = step ^ place_ref[0] if even else jnp.where(far >= expert_count, far - expert_count, far)
        named = jnp.zeros((total, token_rows), F32)
        prob = jnp.zeros((total, token_rows), F32)
        for k in range(top_count):
            hit = ids_ref[k : k + 1, :] == wanted
            named = jnp.where(hit, 1.0, named)
            prob = jnp.where(hit, probs_ref[k : k + 1, :], prob)
        earlier = lax.broadcasted_iota(jnp.int32, (token_rows, token_rows), 0)
        later = lax.broadcasted_iota(jnp.int32, (token_rows, token_rows), 1)
        before = jnp.where(earlier < later, 1.0, 0.0).astype(BF16)
        slot = dot(named.astype(BF16), before)
        own_slot = (row - step * capacity).astype(F32)
        select = jnp.where((named > 0.5) & (slot == own_slot), 1.0, 0.0)
        pick = select.astype(BF16)
        select_ref[...] = pick
        for j in range(dp_count):
            source = pl.ds(pl.multiple_of((place_ref[1] ^ j) * width, width), width)
            target = slice(j * width, (j + 1) * width)
            rows_x = dot(pick, x_ref[:, source]).astype(BF16)
            rows_dy = dot(pick, dy_ref[:, source]).astype(BF16)
            for e in range(expert_count):
                part = slice(e * capacity, (e + 1) * capacity)
                chunks[e][0:capacity, target] = rows_x[part]
                chunks[e][capacity:, target] = rows_dy[part]
        table = (select * prob).T
        high = table.astype(BF16)
        rest = table - high.astype(F32)
        middle = rest.astype(BF16)
        table_ref[:, 0:total] = high
        table_ref[:, total : 2 * total] = middle
        table_ref[:, 2 * total :] = (rest - middle.astype(F32)).astype(BF16)

    outs = [shape((2 * capacity, tokens.shape[1]))] * expert_count
    outs += [shape((total, token_rows)), shape((token_rows, 3 * total))]
    got = call(kernel, outs, place, ids, probs, tokens, cotangent, smem=1)
    return got[:expert_count], got[expert_count], got[expert_count + 1]


def first_half(chunks, pieces, near, width):
    count, dp_count = len(chunks), len(pieces)
    capacity = chunks[0].shape[0] // 2
    total = count * capacity
    model_width = chunks[0].shape[1]
    ff = pieces[0][2].shape[0]
    weights = [w for p in pieces for w in p if w is not None]

    def kernel(*refs):
        chunk_refs, refs = refs[:count], refs[count:]
        weight_refs, (rows_ref, keep_ref, send_ref, sums_ref) = refs[: len(weights)], refs[len(weights) :]
        for e in range(count):
            rows_ref[e * capacity : (e + 1) * capacity, :] = chunk_refs[e][0:capacity, :]
            rows_ref[total + e * capacity : total + (e + 1) * capacity, :] = chunk_refs[e][capacity:, :]
        keep_ref[...] = rows_ref[:, 0 : near * width]
        send_ref[...] = rows_ref[:, near * width :]
        sums = [0.0, 0.0, 0.0, 0.0]
        at = 0
        for j, piece in enumerate(pieces):
            column = slice(j * width, (j + 1) * width)
            x, dy = rows_ref[0:total, column], rows_ref[total:, column]
            if j < near:
                sums[0] += dot(x, weight_refs[at][...])
                sums[1] += dot(x, weight_refs[at + 1][...])
                sums[3] += dot_last(dy, weight_refs[at + 2][...])
                at += 3
            else:
                sums[2] += dot(x, weight_refs[at][...])
                sums[3] += dot_last(dy, weight_refs[at + 1][...])
                at += 2
        for k in range(4):
            sums_ref[:, k * ff : (k + 1) * ff] = sums[k]

    outs = [
        shape((2 * total, model_width)),
        shape((2 * total, near * width)),
        shape((2 * total, model_width - near * width)),
        shape((total, 4 * ff), F32),
    ]
    return call(kernel, outs, *chunks, *weights, weight=FIRST_WEIGHT)


def second_half(flag, rows, sums, pieces, near, width, count):
    total = rows.shape[0] // 2
    capacity = total // count
    model_width = rows.shape[1]
    ff = sums.shape[1] // 4
    weights = [w for p in pieces for w in p]
    far = [j for j in range(len(pieces)) if j >= near]

    def kernel(flag_ref, rows_ref, sums_ref, *refs):
        weight_refs, outs = refs[: len(weights)], refs[len(weights) :]
        chunk_refs, trio_ref = outs[:count], outs[count]
        last = 0.0
        for j in far:
            last += dot(rows_ref[0:total, j * width : (j + 1) * width], weight_refs[3 * j + 1][...])
        lead = sums_ref[:, 2 * ff : 3 * ff]
        swapped = flag_ref[0] != 0
        gate_part = sums_ref[:, 0:ff] + jnp.where(swapped, last, lead)
        up_part = sums_ref[:, ff : 2 * ff] + jnp.where(swapped, lead, last)
        back_hidden = sums_ref[:, 3 * ff :]
        sigmoid_gate = jax.nn.sigmoid(gate_part)
        activated = gate_part * sigmoid_gate
        hidden = (activated * up_part).astype(BF16)
        d_gate = back_hidden * up_part * sigmoid_gate * (1.0 + gate_part * (1.0 - sigmoid_gate))
        d_up = back_hidden * activated
        far_first = jnp.where(swapped, d_up, d_gate).astype(BF16)
        far_second = jnp.where(swapped, d_gate, d_up).astype(BF16)
        d_gate, d_up = d_gate.astype(BF16), d_up.astype(BF16)
        trio_ref[:, 0:ff] = hidden
        trio_ref[:, ff : 2 * ff] = d_gate
        trio_ref[:, 2 * ff :] = d_up
        for j in range(len(pieces)):
            column = slice(j * width, (j + 1) * width)
            one, two = (d_gate, d_up) if j < near else (far_first, far_second)
            out = dot(hidden, weight_refs[3 * j + 2][...]).astype(BF16)
            back = dot_last(one, weight_refs[3 * j][...]) + dot_last(two, weight_refs[3 * j + 1][...])
            back = back.astype(BF16)
            for e in range(count):
                part = slice(e * capacity, (e + 1) * capacity)
                chunk_refs[e][0:capacity, column] = out[part]
                chunk_refs[e][capacity:, column] = back[part]

    outs = [shape((2 * capacity, model_width))] * count + [shape((total, 3 * ff))]
    got = call(kernel, outs, flag, rows, sums, *weights, smem=1)
    return got[:count], got[count]


def gradients(keeps, trios, width, ff):
    count = len(keeps)

    def kernel(*refs):
        keep_refs, trio_refs = refs[:count], refs[count : 2 * count]
        gate_ref, up_ref, down_ref = refs[2 * count :]
        half = keep_refs[0].shape[0] // 2
        x = jnp.concatenate([r[0:half, 0:width] for r in keep_refs], axis=0)
        dy = jnp.concatenate([r[half:, 0:width] for r in keep_refs], axis=0)
        trio = jnp.concatenate([r[...] for r in trio_refs], axis=0)
        gate_ref[...] = dot_first(x, trio[:, ff : 2 * ff]).astype(BF16)
        up_ref[...] = dot_first(x, trio[:, 2 * ff :]).astype(BF16)
        down_ref[...] = dot_first(trio[:, 0:ff], dy).astype(BF16)

    outs = [shape((width, ff)), shape((width, ff)), shape((ff, width))]
    return call(kernel, outs, *keeps, *trios)


def collect(place, ids, select, table, cotangent, chunks, dp_count, even):
    count = len(chunks)
    capacity = chunks[0].shape[0] // 2
    total = count * capacity
    token_rows, model_width = cotangent.shape
    width = model_width // dp_count

    def kernel(place_ref, ids_ref, select_ref, table_ref, dy_ref, *refs):
        chunk_refs, (mixed_ref, grad_ref, gates_ref) = refs[:count], refs[count:]
        inner = 0.0
        for j in range(dp_count):
            column = slice(j * width, (j + 1) * width)
            home = pl.ds(pl.multiple_of((place_ref[1] ^ j) * width, width), width)
            out = jnp.concatenate([r[0:capacity, column] for r in chunk_refs], axis=0)
            back = jnp.concatenate([r[capacity:, column] for r in chunk_refs], axis=0)
            mixed_ref[:, home] = dot(table_ref[...], jnp.concatenate([out] * 3, axis=0)).astype(BF16)
            grad_ref[:, home] = dot(table_ref[...], jnp.concatenate([back] * 3, axis=0)).astype(BF16)
            inner += dot_last(out, dy_ref[:, home])
        inner = jnp.where(select_ref[...] > 0, inner, 0.0)
        step = lax.broadcasted_iota(jnp.int32, (total, token_rows), 0) // capacity
        far = step + place_ref[0]
        wanted = step ^ place_ref[0] if even else jnp.where(far >= count, far - count, far)
        for k in range(ids_ref.shape[0]):
            hit = ids_ref[k : k + 1, :] == wanted
            gates_ref[k : k + 1, :] = jnp.sum(jnp.where(hit, inner, 0.0), axis=0, keepdims=True)

    outs = [
        shape((token_rows, model_width)),
        shape((token_rows, model_width)),
        shape(ids.shape, F32),
    ]
    return call(
        kernel, outs, place, ids, select, table, cotangent, *chunks, smem=1, weight=COLLECT_WEIGHT
    )


def on_device(tokens, cotangent, expert_ids, gate_probs, w_gate, w_up, w_down):
    expert_count = lax.axis_size("expert")
    dp_count = lax.axis_size("dp")
    token_rows = tokens.shape[0]
    width, ff = w_gate.shape[1:]
    capacity = 2 * token_rows * expert_ids.shape[1] // EXPERTS
    group = lax.axis_index("groups").astype(jnp.int32)
    place = jnp.stack([lax.axis_index("expert"), lax.axis_index("dp")]).astype(jnp.int32)
    even = expert_count & (expert_count - 1) == 0
    paired = lax.axis_size("groups") == 2
    flag = (group if paired else jnp.zeros_like(group)).reshape(1)

    def to_dp(array, mask):
        return lax.ppermute(array, "dp", [(i, i ^ mask) for i in range(dp_count)])

    def to_group(array):
        return lax.ppermute(array, "groups", [(0, 1), (1, 0)])

    def to_expert(array, step):
        if even:
            pairs = [(i, i ^ step) for i in range(expert_count)]
        else:
            pairs = [(i, (i + step) % expert_count) for i in range(expert_count)]
        return lax.ppermute(array, "expert", pairs)

    def after(values, *others):
        return lax.optimization_barrier((values, others))[0]

    own = (w_gate[0], w_up[0], w_down[0])
    lead = choose(group, own[0], own[1]) if paired else own[0]
    own = after(own, lead)
    masks = range(CORES, dp_count, CORES)
    lead_got = {mask: to_dp(lead, mask) for mask in masks}
    other_got = {
        mask: to_group(lead_got[mask]) if paired else to_dp(own[1], mask) for mask in masks
    }
    sibling = tuple(to_dp(w, 1) for w in own)

    ids, probs = expert_ids.T, gate_probs.T
    send, select, table = slots(
        place, ids, probs, tokens, cotangent, expert_count, capacity, dp_count, even
    )
    order = [1, *range(expert_count - 1, 1, -1)]
    send = after(send, sibling)
    down = after(own[2], send)
    down_got = {mask: to_dp(down, mask) for mask in masks}
    got = [send[0]] + [None] * (expert_count - 1)
    for j in order:
        got[j] = to_expert(send[j], j)

    early = [(own[0], own[1], own[2]), (sibling[0], sibling[1], sibling[2])]
    full = list(early)
    for mask in masks:
        lead_sib, down_sib = (to_dp(after(w, got), 1) for w in (lead_got[mask], down_got[mask]))
        early += [(lead_got[mask], None, down_got[mask]), (lead_sib, None, down_sib)]
        other_sib = to_dp(other_got[mask], 1)
        full += [
            (lead_got[mask], other_got[mask], down_got[mask]),
            (lead_sib, other_sib, down_sib),
        ]
    rows, keep, far_rows, sums = first_half(got, early, CORES, width)
    back, trio = second_half(flag, rows, sums, full, CORES, width, expert_count)

    home = [back[0]] + [None] * (expert_count - 1)
    for j in order:
        home[j] = to_expert(back[j], j if even else -j)

    kept = [keep]
    for i, mask in enumerate(masks):
        part = far_rows[:, i * CORES * width : (i + 1) * CORES * width]
        kept.append(to_dp(part, mask))
    trios = [trio] + [to_dp(trio, mask) for mask in masks]
    trios, kept = lax.optimization_barrier((trios, kept))
    theirs = to_dp(jnp.concatenate([k[:, width:] for k in kept], axis=0), 1)
    size = keep.shape[0]
    kept += [theirs[i * size : (i + 1) * size] for i in range(len(kept))]
    trios += [to_dp(t, 1) for t in trios]

    mixed, grad_tokens, grad_gates = collect(
        place, ids, select, table, cotangent, home, dp_count, even
    )
    mixed, kept, trios = lax.optimization_barrier((mixed, kept, trios))
    grad_w_gate, grad_w_up, grad_w_down = gradients(kept, trios, width, ff)
    return (
        mixed,
        grad_tokens,
        grad_gates.T,
        grad_w_gate[None],
        grad_w_up[None],
        grad_w_down[None],
    )


def solution(mesh):
    rows = P(("groups", "expert", "dp"), None)
    in_specs = (
        rows,
        rows,
        rows,
        rows,
        P("expert", "dp", None),
        P("expert", "dp", None),
        P("expert", None, "dp"),
    )
    out_specs = (
        rows,
        rows,
        rows,
        P(("groups", "expert"), "dp", None),
        P(("groups", "expert"), "dp", None),
        P(("groups", "expert"), None, "dp"),
    )
    return jax.shard_map(
        on_device, mesh=mesh, in_specs=in_specs, out_specs=out_specs, check_vma=False
    )
```

```python
import jax
import jax.numpy as jnp
from jax import lax
from jax.experimental import pallas as pl
from jax.experimental.pallas import tpu as pltpu
from jax.sharding import PartitionSpec as P

EXPERTS = 128
CORES = 2
BF16 = jnp.bfloat16
F32 = jnp.float32
VMEM_LIMIT = 16 << 20
FIRST_WEIGHT = 9 * 10**9
COLLECT_WEIGHT = 1 << 33
BACK_WEIGHT = 1 << 33


def dot(left, right):
    return jnp.dot(left, right, preferred_element_type=F32)


def dot_first(left, right):
    return lax.dot_general(left, right, (((0,), (0,)), ((), ())), preferred_element_type=F32)


def dot_last(left, right):
    return lax.dot_general(left, right, (((1,), (1,)), ((), ())), preferred_element_type=F32)


def shape(dims, dtype=BF16):
    return jax.ShapeDtypeStruct(dims, dtype)


def call(kernel, out_shape, *args, smem=0, scratch=(), flops=0, anywhere=(), weight=1):
    vmem = pl.BlockSpec(memory_space=pltpu.VMEM)
    args = [
        pltpu.with_memory_space_constraint(a, pltpu.HBM) if i in anywhere else a
        for i, a in enumerate(args)
    ]
    specs = [
        pl.BlockSpec(memory_space=pltpu.SMEM)
        if i < smem
        else pl.BlockSpec(memory_space=pl.ANY)
        if i in anywhere
        else vmem
        for i in range(len(args))
    ]
    return pl.pallas_call(
        kernel,
        out_shape=out_shape,
        in_specs=specs,
        out_specs=jax.tree.map(lambda _: vmem, out_shape),
        scratch_shapes=list(scratch),
        compiler_params=pltpu.CompilerParams(vmem_limit_bytes=VMEM_LIMIT),
        cost_estimate=pl.CostEstimate(flops=weight, bytes_accessed=1, transcendentals=0),
    )(*args)


def step_of(index, count):
    return jnp.where(index == 0, 0, count - index) if isinstance(index, jax.Array) else -index % count


def choose(flag, first, second):
    rows, columns = first.shape

    def kernel(flag_ref, first_ref, second_ref, one_ref, both_ref, sems):
        top = pltpu.make_async_copy(first_ref, both_ref.at[0:rows], sems.at[0])
        bottom = pltpu.make_async_copy(second_ref, both_ref.at[rows:], sems.at[1])
        top.start()
        bottom.start()

        @pl.when(flag_ref[0] == 0)
        def _():
            copy = pltpu.make_async_copy(first_ref, one_ref, sems.at[2])
            copy.start()
            copy.wait()

        @pl.when(flag_ref[0] != 0)
        def _():
            copy = pltpu.make_async_copy(second_ref, one_ref, sems.at[2])
            copy.start()
            copy.wait()

        top.wait()
        bottom.wait()

    return call(
        kernel,
        [shape((rows, columns)), shape((2 * rows, columns))],
        flag,
        first,
        second,
        smem=1,
        anywhere=(1, 2),
        scratch=[pltpu.SemaphoreType.DMA((3,))],
    )


def slots(place, ids, probs, tokens, cotangent, expert_count, capacity, dp_count, even):
    top_count, token_rows = ids.shape
    width = tokens.shape[1] // dp_count
    total = expert_count * capacity

    def kernel(place_ref, ids_ref, probs_ref, x_hbm, dy_hbm, *outs):
        chunks, outs = outs[:expert_count], outs[expert_count:]
        select_ref, table_ref, x_ref, dy_ref, sems = outs
        copies = []
        for j in range(dp_count):
            source = pl.ds(pl.multiple_of((place_ref[1] ^ j) * width, width), width)
            target = pl.ds(j * width, width)
            for i, (hbm, ref) in enumerate(((x_hbm, x_ref), (dy_hbm, dy_ref))):
                copy = pltpu.make_async_copy(hbm.at[:, source], ref.at[:, target], sems.at[2 * j + i])
                copy.start()
                copies.append(copy)
        row = lax.broadcasted_iota(jnp.int32, (total, token_rows), 0)
        step = step_of(row // capacity, expert_count)
        far = step + place_ref[0]
        wanted = step ^ place_ref[0] if even else jnp.where(far >= expert_count, far - expert_count, far)
        named = jnp.zeros((total, token_rows), F32)
        prob = jnp.zeros((total, token_rows), F32)
        for k in range(top_count):
            hit = ids_ref[k : k + 1, :] == wanted
            named = jnp.where(hit, 1.0, named)
            prob = jnp.where(hit, probs_ref[k : k + 1, :], prob)
        earlier = lax.broadcasted_iota(jnp.int32, (token_rows, token_rows), 0)
        later = lax.broadcasted_iota(jnp.int32, (token_rows, token_rows), 1)
        before = jnp.where(earlier < later, 1.0, 0.0).astype(BF16)
        slot = dot(named.astype(BF16), before)
        own_slot = (row % capacity).astype(F32)
        select = jnp.where((named > 0.5) & (slot == own_slot), 1.0, 0.0)
        pick = select.astype(BF16)
        select_ref[...] = pick
        for j in range(dp_count):
            target = slice(j * width, (j + 1) * width)
            copies[2 * j].wait()
            copies[2 * j + 1].wait()
            rows_x = dot(pick, x_ref[:, target]).astype(BF16)
            rows_dy = dot(pick, dy_ref[:, target]).astype(BF16)
            for e in range(expert_count):
                part = slice(e * capacity, (e + 1) * capacity)
                chunks[e][0:capacity, target] = rows_x[part]
                chunks[e][capacity:, target] = rows_dy[part]
        table = (select * prob).T
        high = table.astype(BF16)
        rest = table - high.astype(F32)
        middle = rest.astype(BF16)
        table_ref[:, 0:total] = high
        table_ref[:, total : 2 * total] = middle
        table_ref[:, 2 * total :] = (rest - middle.astype(F32)).astype(BF16)

    outs = [shape((2 * capacity, tokens.shape[1]))] * expert_count
    outs += [shape((total, token_rows)), shape((token_rows, 3 * total))]
    got = call(
        kernel,
        outs,
        place,
        ids,
        probs,
        tokens,
        cotangent,
        smem=1,
        anywhere=(3, 4),
        scratch=[
            pltpu.VMEM(tokens.shape, BF16),
            pltpu.VMEM(tokens.shape, BF16),
            pltpu.SemaphoreType.DMA((2 * dp_count,)),
        ],
    )
    return got[:expert_count], got[expert_count], got[expert_count + 1]


def arrange(chunks, dp_count, near):
    count = len(chunks)
    capacity, model_width = chunks[0].shape[0] // 2, chunks[0].shape[1]
    total = count * capacity
    width = model_width // dp_count * near
    dp_count //= near

    def kernel(*refs):
        chunk_refs, rows_ref, part_refs = refs[:count], refs[count], refs[count + 1 :]
        for e in range(count):
            x, dy = slice(e * capacity, (e + 1) * capacity), slice(total + e * capacity, total + (e + 1) * capacity)
            rows_ref[x, :] = chunk_refs[e][0:capacity, :]
            rows_ref[dy, :] = chunk_refs[e][capacity:, :]
            for j in range(dp_count):
                column = slice(j * width, (j + 1) * width)
                part_refs[j][x, :] = chunk_refs[e][0:capacity, column]
                part_refs[j][dy, :] = chunk_refs[e][capacity:, column]

    outs = [shape((2 * total, model_width))] + [shape((2 * total, width))] * dp_count
    got = call(kernel, outs, *chunks)
    return got[0], got[1:]


def first_half(rows, near_pieces, far_leads, width):
    total = rows.shape[0] // 2
    ff = near_pieces[0][1].shape[0]
    near = len(near_pieces)
    given = [(j, w) for j, w in enumerate(far_leads) if w is not None]
    weights = [w for p in near_pieces for w in p] + [w for _, w in given]

    def kernel(rows_ref, *refs):
        weight_refs, sums_ref = refs[:-1], refs[-1]
        sums = [0.0, 0.0, 0.0, 0.0]
        for j in range(near):
            column = slice(j * width, (j + 1) * width)
            x, dy = rows_ref[0:total, column], rows_ref[total:, column]
            sums[0] += dot(x, weight_refs[2 * j][0:width, :])
            sums[1] += dot(x, weight_refs[2 * j][width:, :])
            sums[3] += dot_last(dy, weight_refs[2 * j + 1][...])
        for i, (j, _) in enumerate(given):
            x = rows_ref[0:total, (near + j) * width : (near + j + 1) * width]
            sums[2] += dot(x, weight_refs[2 * near + i][...])
        for k in range(4):
            sums_ref[:, k * ff : (k + 1) * ff] = sums[k]

    return call(kernel, shape((total, 4 * ff), F32), rows, *weights, weight=FIRST_WEIGHT)


def far_sums(rows, sums, leads, downs, near, width):
    total = rows.shape[0] // 2
    ff = sums.shape[1] // 4
    given = [(j, w) for j, w in enumerate(leads) if w is not None]

    def kernel(rows_ref, sums_ref, *refs):
        lead_refs, down_refs, out_ref = refs[: len(given)], refs[len(given) : -1], refs[-1]
        lead = sums_ref[:, 2 * ff : 3 * ff]
        back_hidden = sums_ref[:, 3 * ff :]
        for (j, _), ref in zip(given, lead_refs):
            lead += dot(rows_ref[0:total, (near + j) * width : (near + j + 1) * width], ref[...])
        for j, ref in enumerate(down_refs):
            column = slice((near + j) * width, (near + j + 1) * width)
            back_hidden += dot_last(rows_ref[total:, column], ref[...])
        out_ref[:, 0:ff] = lead
        out_ref[:, ff:] = back_hidden

    return call(
        kernel,
        shape((total, 2 * ff), F32),
        rows,
        sums,
        *(w for _, w in given),
        *downs,
        weight=BACK_WEIGHT,
    )


def second_half(flag, rows, sums, far, near_pieces, far_pieces, width, count):
    total = rows.shape[0] // 2
    capacity = total // count
    model_width = rows.shape[1]
    ff = sums.shape[1] // 4
    near = len(near_pieces)
    weights = [w for p in (*near_pieces, *far_pieces) for w in p]

    def kernel(flag_ref, rows_ref, sums_ref, back_ref, *refs):
        weight_refs, outs = refs[: len(weights)], refs[len(weights) :]
        chunk_refs, trio_ref = outs[:count], outs[count]
        far_refs = [weight_refs[2 * near + 3 * j : 2 * near + 3 * j + 3] for j in range(len(far_pieces))]
        last, back_hidden = 0.0, back_ref[:, ff:]
        for j, (_, late, _) in enumerate(far_refs):
            column = slice((near + j) * width, (near + j + 1) * width)
            last += dot(rows_ref[0:total, column], late[...])
        lead = back_ref[:, 0:ff]
        swapped = flag_ref[0] != 0
        gate_part = sums_ref[:, 0:ff] + jnp.where(swapped, last, lead)
        up_part = sums_ref[:, ff : 2 * ff] + jnp.where(swapped, lead, last)
        sigmoid_gate = jax.nn.sigmoid(gate_part)
        activated = gate_part * sigmoid_gate
        hidden = (activated * up_part).astype(BF16)
        d_gate = back_hidden * up_part * sigmoid_gate * (1.0 + gate_part * (1.0 - sigmoid_gate))
        d_up = back_hidden * activated
        far_first = jnp.where(swapped, d_up, d_gate).astype(BF16)
        far_second = jnp.where(swapped, d_gate, d_up).astype(BF16)
        d_gate, d_up = d_gate.astype(BF16), d_up.astype(BF16)
        trio_ref[:, 0:ff] = hidden
        trio_ref[:, ff : 2 * ff] = d_gate
        trio_ref[:, 2 * ff :] = d_up
        for j in range(near + len(far_pieces)):
            column = slice(j * width, (j + 1) * width)
            if j < near:
                down = weight_refs[2 * j + 1]
                back = dot_last(d_gate, weight_refs[2 * j][0:width, :])
                back += dot_last(d_up, weight_refs[2 * j][width:, :])
            else:
                one, two, down = far_refs[j - near]
                back = dot_last(far_first, one[...]) + dot_last(far_second, two[...])
            out = dot(hidden, down[...]).astype(BF16)
            back = back.astype(BF16)
            for e in range(count):
                part = slice(e * capacity, (e + 1) * capacity)
                chunk_refs[e][0:capacity, column] = out[part]
                chunk_refs[e][capacity:, column] = back[part]

    outs = [shape((2 * capacity, model_width))] * count + [shape((total, 3 * ff))]
    got = call(kernel, outs, flag, rows, sums, far, *weights, smem=1)
    return got[:count], got[count]


def gradients(keeps, trios, width, ff):
    count = len(keeps)

    def kernel(*refs):
        keep_refs, trio_refs = refs[:count], refs[count : 2 * count]
        gate_ref, up_ref, down_ref = refs[2 * count :]
        half = keep_refs[0].shape[0] // 2
        x = jnp.concatenate([r[0:half, 0:width] for r in keep_refs], axis=0)
        dy = jnp.concatenate([r[half:, 0:width] for r in keep_refs], axis=0)
        trio = jnp.concatenate([r[...] for r in trio_refs], axis=0)
        gate_ref[...] = dot_first(x, trio[:, ff : 2 * ff]).astype(BF16)
        up_ref[...] = dot_first(x, trio[:, 2 * ff :]).astype(BF16)
        down_ref[...] = dot_first(trio[:, 0:ff], dy).astype(BF16)

    outs = [shape((width, ff)), shape((width, ff)), shape((ff, width))]
    return call(kernel, outs, *keeps, *trios)


def collect(place, ids, select, table, cotangent, chunks, dp_count, even):
    count = len(chunks)
    capacity = chunks[0].shape[0] // 2
    total = count * capacity
    token_rows, model_width = cotangent.shape
    width = model_width // dp_count

    def kernel(place_ref, ids_ref, select_ref, table_ref, dy_ref, *refs):
        chunk_refs, (mixed_ref, grad_ref, gates_ref) = refs[:count], refs[count:]
        inner = 0.0
        for j in range(dp_count):
            column = slice(j * width, (j + 1) * width)
            home = pl.ds(pl.multiple_of((place_ref[1] ^ j) * width, width), width)
            out = jnp.concatenate([r[0:capacity, column] for r in chunk_refs], axis=0)
            back = jnp.concatenate([r[capacity:, column] for r in chunk_refs], axis=0)
            mixed_ref[:, home] = dot(table_ref[...], jnp.concatenate([out] * 3, axis=0)).astype(BF16)
            grad_ref[:, home] = dot(table_ref[...], jnp.concatenate([back] * 3, axis=0)).astype(BF16)
            inner += dot_last(out, dy_ref[:, home])
        inner = jnp.where(select_ref[...] > 0, inner, 0.0)
        step = step_of(lax.broadcasted_iota(jnp.int32, (total, token_rows), 0) // capacity, count)
        far = step + place_ref[0]
        wanted = step ^ place_ref[0] if even else jnp.where(far >= count, far - count, far)
        for k in range(ids_ref.shape[0]):
            hit = ids_ref[k : k + 1, :] == wanted
            gates_ref[k : k + 1, :] = jnp.sum(jnp.where(hit, inner, 0.0), axis=0, keepdims=True)

    outs = [
        shape((token_rows, model_width)),
        shape((token_rows, model_width)),
        shape(ids.shape, F32),
    ]
    return call(
        kernel, outs, place, ids, select, table, cotangent, *chunks, smem=1, weight=COLLECT_WEIGHT
    )


def on_device(tokens, cotangent, expert_ids, gate_probs, w_gate, w_up, w_down):
    expert_count = lax.axis_size("expert")
    dp_count = lax.axis_size("dp")
    token_rows = tokens.shape[0]
    width, ff = w_gate.shape[1:]
    capacity = 2 * token_rows * expert_ids.shape[1] // EXPERTS
    group = lax.axis_index("groups").astype(jnp.int32)
    place = jnp.stack([lax.axis_index("expert"), lax.axis_index("dp")]).astype(jnp.int32)
    even = expert_count & (expert_count - 1) == 0
    paired = lax.axis_size("groups") == 2
    flag = (group if paired else jnp.zeros_like(group)).reshape(1)

    def to_dp(array, mask):
        return lax.ppermute(array, "dp", [(i, i ^ mask) for i in range(dp_count)])

    def to_group(array):
        return lax.ppermute(array, "groups", [(0, 1), (1, 0)])

    def to_expert(array, step):
        if even:
            pairs = [(i, i ^ step) for i in range(expert_count)]
        else:
            pairs = [(i, (i + step) % expert_count) for i in range(expert_count)]
        return lax.ppermute(array, "expert", pairs)

    def after(values, *others):
        return lax.optimization_barrier((values, others))[0]

    lead, both = choose(flag, w_gate[0], w_up[0])
    down = after(w_down[0], lead)
    masks = range(CORES, dp_count, CORES)
    lead_got = {mask: to_dp(lead, mask) for mask in masks}
    near_pieces = [(both, down), (to_dp(both, 1), to_dp(down, 1))]

    ids, probs = expert_ids.T, gate_probs.T
    send, select, table = slots(
        place, ids, probs, tokens, cotangent, expert_count, capacity, dp_count, even
    )
    send, down_far = after((send, down), near_pieces[1])
    down_got = {mask: to_dp(down_far, mask) for mask in masks}
    lead_got = after(lead_got, send)
    if paired:
        late_got = {mask: to_group(lead_got[mask]) for mask in masks}
    else:
        late_got = {mask: to_dp(w_up[0], mask) for mask in masks}
    ways = [step_of(i, expert_count) for i in range(expert_count)]
    got = [send[0]] + [to_expert(c, j) for c, j in zip(send[1:], ways[1:])]

    rows, parts = arrange(got, dp_count, CORES)
    lead_sib = {mask: to_dp(lead_got[mask], 1) for mask in masks}
    far_leads = [w for mask in masks for w in (lead_got[mask], None)]
    sums = first_half(rows, near_pieces, far_leads, width)
    late_got = after(late_got, sums)
    far_pieces = []
    for mask in masks:
        late_sib, down_sib = to_dp(late_got[mask], 1), to_dp(down_got[mask], 1)
        far_pieces += [
            (lead_got[mask], late_got[mask], down_got[mask]),
            (lead_sib[mask], late_sib, down_sib),
        ]
    far = far_sums(
        rows,
        sums,
        [w for mask in masks for w in (None, lead_sib[mask])],
        [p[2] for p in far_pieces],
        CORES,
        width,
    )
    back, trio = second_half(
        flag, rows, sums, far, near_pieces, far_pieces, width, expert_count
    )

    home = [back[0]]
    home += [to_expert(c, j if even else -j) for c, j in zip(back[1:], ways[1:])]
    peers = [*masks, 1, *(mask + 1 for mask in masks)]
    trios = [trio] + [to_dp(trio, j) for j in peers]
    parts = after(parts, trio)
    kept = [parts[0]] + [to_dp(parts[i + 1], mask) for i, mask in enumerate(masks)]
    theirs = to_dp(jnp.concatenate([k[:, width:] for k in kept], axis=0), 1)
    size = rows.shape[0]
    kept += [theirs[i * size : (i + 1) * size] for i in range(len(kept))]
    mixed, grad_tokens, grad_gates = collect(
        place, ids, select, table, cotangent, home, dp_count, even
    )
    mixed, kept, trios = lax.optimization_barrier((mixed, kept, trios))
    grad_w_gate, grad_w_up, grad_w_down = gradients(kept, trios, width, ff)
    return (
        mixed,
        grad_tokens,
        grad_gates.T,
        grad_w_gate[None],
        grad_w_up[None],
        grad_w_down[None],
    )


def solution(mesh):
    rows = P(("groups", "expert", "dp"), None)
    in_specs = (
        rows,
        rows,
        rows,
        rows,
        P("expert", "dp", None),
        P("expert", "dp", None),
        P("expert", None, "dp"),
    )
    out_specs = (
        rows,
        rows,
        rows,
        P(("groups", "expert"), "dp", None),
        P(("groups", "expert"), "dp", None),
        P(("groups", "expert"), None, "dp"),
    )
    return jax.shard_map(
        on_device, mesh=mesh, in_specs=in_specs, out_specs=out_specs, check_vma=False
    )
```

```python
import jax
import jax.numpy as jnp
from jax import lax
from jax.experimental import pallas as pl
from jax.experimental.pallas import tpu as pltpu
from jax.sharding import PartitionSpec as P

EXPERTS = 128
CORES = 2
BF16 = jnp.bfloat16
F32 = jnp.float32
VMEM_LIMIT = 16 << 20
FIRST_WEIGHT = 9 * 10**9
COLLECT_WEIGHT = 1 << 33
BACK_WEIGHT = 1 << 33


def dot(left, right):
    return jnp.dot(left, right, preferred_element_type=F32)


def dot_first(left, right):
    return lax.dot_general(left, right, (((0,), (0,)), ((), ())), preferred_element_type=F32)


def dot_last(left, right):
    return lax.dot_general(left, right, (((1,), (1,)), ((), ())), preferred_element_type=F32)


def shape(dims, dtype=BF16):
    return jax.ShapeDtypeStruct(dims, dtype)


def call(kernel, out_shape, *args, smem=0, scratch=(), anywhere=(), weight=1):
    vmem = pl.BlockSpec(memory_space=pltpu.VMEM)
    args = [
        pltpu.with_memory_space_constraint(a, pltpu.HBM) if i in anywhere else a
        for i, a in enumerate(args)
    ]
    specs = [
        pl.BlockSpec(memory_space=pltpu.SMEM)
        if i < smem
        else pl.BlockSpec(memory_space=pl.ANY)
        if i in anywhere
        else vmem
        for i in range(len(args))
    ]
    return pl.pallas_call(
        kernel,
        out_shape=out_shape,
        in_specs=specs,
        out_specs=jax.tree.map(lambda _: vmem, out_shape),
        scratch_shapes=list(scratch),
        compiler_params=pltpu.CompilerParams(vmem_limit_bytes=VMEM_LIMIT),
        cost_estimate=pl.CostEstimate(flops=weight, bytes_accessed=1, transcendentals=0),
    )(*args)


def step_of(index, count):
    step = 1 + (index + count // 2 - 2) % max(count - 1, 1)
    return jnp.where(index == 0, 0, step) if isinstance(index, jax.Array) else step * (index > 0)


def choose(flag, first, second):
    rows, columns = first.shape

    def kernel(flag_ref, first_ref, second_ref, one_ref, both_ref, sems):
        top = pltpu.make_async_copy(first_ref, both_ref.at[0:rows], sems.at[0])
        bottom = pltpu.make_async_copy(second_ref, both_ref.at[rows:], sems.at[1])
        top.start()
        bottom.start()

        @pl.when(flag_ref[0] == 0)
        def _():
            copy = pltpu.make_async_copy(first_ref, one_ref, sems.at[2])
            copy.start()
            copy.wait()

        @pl.when(flag_ref[0] != 0)
        def _():
            copy = pltpu.make_async_copy(second_ref, one_ref, sems.at[2])
            copy.start()
            copy.wait()

        top.wait()
        bottom.wait()

    return call(
        kernel,
        [shape((rows, columns)), shape((2 * rows, columns))],
        flag,
        first,
        second,
        smem=1,
        anywhere=(1, 2),
        scratch=[pltpu.SemaphoreType.DMA((3,))],
    )


def slots(place, ids, probs, tokens, cotangent, expert_count, capacity, dp_count, even):
    top_count, token_rows = ids.shape
    width = tokens.shape[1] // dp_count
    total = expert_count * capacity

    def kernel(place_ref, ids_ref, probs_ref, x_ref, dy_hbm, *outs):
        chunks, (select_ref, table_ref, dy_ref, sem) = outs[:expert_count], outs[expert_count:]
        fetch = pltpu.make_async_copy(dy_hbm, dy_ref, sem)
        fetch.start()
        row = lax.broadcasted_iota(jnp.int32, (total, token_rows), 0)
        step = step_of(row // capacity, expert_count)
        far = step + place_ref[0]
        wanted = step ^ place_ref[0] if even else jnp.where(far >= expert_count, far - expert_count, far)
        named = jnp.zeros((total, token_rows), F32)
        prob = jnp.zeros((total, token_rows), F32)
        for k in range(top_count):
            hit = ids_ref[k : k + 1, :] == wanted
            named = jnp.where(hit, 1.0, named)
            prob = jnp.where(hit, probs_ref[k : k + 1, :], prob)
        earlier = lax.broadcasted_iota(jnp.int32, (token_rows, token_rows), 0)
        later = lax.broadcasted_iota(jnp.int32, (token_rows, token_rows), 1)
        before = jnp.where(earlier < later, 1.0, 0.0).astype(BF16)
        slot = dot(named.astype(BF16), before)
        own_slot = (row % capacity).astype(F32)
        select = jnp.where((named > 0.5) & (slot == own_slot), 1.0, 0.0)
        pick = select.astype(BF16)
        select_ref[...] = pick
        def gather(ref, first):
            for j in range(dp_count):
                source = pl.ds(pl.multiple_of((place_ref[1] ^ j) * width, width), width)
                got = dot(pick, ref[:, source]).astype(BF16)
                for e in range(expert_count):
                    chunks[e][first : first + capacity, j * width : (j + 1) * width] = got[
                        e * capacity : (e + 1) * capacity
                    ]

        gather(x_ref, 0)
        table = (select * prob).T
        high = table.astype(BF16)
        table_ref[:, 0:total] = high
        table_ref[:, total:] = (table - high.astype(F32)).astype(BF16)
        fetch.wait()
        gather(dy_ref, capacity)

    outs = [shape((2 * capacity, tokens.shape[1]))] * expert_count
    outs += [shape((total, token_rows)), shape((token_rows, 2 * total))]
    got = call(
        kernel,
        outs,
        place,
        ids,
        probs,
        tokens,
        cotangent,
        smem=1,
        anywhere=(4,),
        scratch=[pltpu.VMEM(cotangent.shape, BF16), pltpu.SemaphoreType.DMA],
    )
    return got[:expert_count], got[expert_count], got[expert_count + 1]


def arrange(chunks, dp_count, near):
    count = len(chunks)
    capacity, model_width = chunks[0].shape[0] // 2, chunks[0].shape[1]
    total = count * capacity
    width = model_width // dp_count * near
    dp_count //= near

    def kernel(*refs):
        chunk_refs, rows_ref, part_refs = refs[:count], refs[count], refs[count + 1 :]
        for e in range(count):
            x, dy = slice(e * capacity, (e + 1) * capacity), slice(total + e * capacity, total + (e + 1) * capacity)
            rows_ref[x, :] = chunk_refs[e][0:capacity, :]
            rows_ref[dy, :] = chunk_refs[e][capacity:, :]
            for j in range(dp_count):
                column = slice(j * width, (j + 1) * width)
                part_refs[j][x, :] = chunk_refs[e][0:capacity, column]
                part_refs[j][dy, :] = chunk_refs[e][capacity:, column]

    outs = [shape((2 * total, model_width))] + [shape((2 * total, width))] * dp_count
    got = call(kernel, outs, *chunks)
    return got[0], got[1:]


def first_half(rows, near_pieces, far_leads, width):
    total = rows.shape[0] // 2
    ff = near_pieces[0][1].shape[0]
    near = len(near_pieces)
    given = [(j, w) for j, w in enumerate(far_leads) if w is not None]
    weights = [w for p in near_pieces for w in p] + [w for _, w in given]

    def kernel(rows_ref, *refs):
        weight_refs, sums_ref = refs[:-1], refs[-1]
        sums = [0.0, 0.0, 0.0, 0.0]
        for j in range(near):
            column = slice(j * width, (j + 1) * width)
            x, dy = rows_ref[0:total, column], rows_ref[total:, column]
            sums[0] += dot(x, weight_refs[2 * j][0:width, :])
            sums[1] += dot(x, weight_refs[2 * j][width:, :])
            sums[3] += dot_last(dy, weight_refs[2 * j + 1][...])
        for i, (j, _) in enumerate(given):
            x = rows_ref[0:total, (near + j) * width : (near + j + 1) * width]
            sums[2] += dot(x, weight_refs[2 * near + i][...])
        for k in range(4):
            sums_ref[:, k * ff : (k + 1) * ff] = sums[k]

    return call(kernel, shape((total, 4 * ff), F32), rows, *weights, weight=FIRST_WEIGHT)


def far_sums(rows, sums, leads, downs, near, width):
    total = rows.shape[0] // 2
    ff = sums.shape[1] // 4
    given = [(j, w) for j, w in enumerate(leads) if w is not None]

    def kernel(rows_ref, sums_ref, *refs):
        lead_refs, down_refs, out_ref = refs[: len(given)], refs[len(given) : -1], refs[-1]
        lead = sums_ref[:, 2 * ff : 3 * ff]
        back_hidden = sums_ref[:, 3 * ff :]
        for (j, _), ref in zip(given, lead_refs):
            lead += dot(rows_ref[0:total, (near + j) * width : (near + j + 1) * width], ref[...])
        for j, ref in enumerate(down_refs):
            column = slice((near + j) * width, (near + j + 1) * width)
            back_hidden += dot_last(rows_ref[total:, column], ref[...])
        out_ref[:, 0:ff] = lead
        out_ref[:, ff:] = back_hidden

    return call(
        kernel,
        shape((total, 2 * ff), F32),
        rows,
        sums,
        *(w for _, w in given),
        *downs,
        weight=BACK_WEIGHT,
    )


def second_half(flag, rows, sums, far, near_pieces, far_pieces, width, count):
    total = rows.shape[0] // 2
    capacity = total // count
    model_width = rows.shape[1]
    ff = sums.shape[1] // 4
    near = len(near_pieces)
    weights = [w for p in (*near_pieces, *far_pieces) for w in p]

    def kernel(flag_ref, rows_ref, sums_ref, back_ref, *refs):
        weight_refs, outs = refs[: len(weights)], refs[len(weights) :]
        chunk_refs, trio_ref = outs[:count], outs[count]
        far_refs = [weight_refs[2 * near + 3 * j : 2 * near + 3 * j + 3] for j in range(len(far_pieces))]
        last, back_hidden = 0.0, back_ref[:, ff:]
        for j, (_, late, _) in enumerate(far_refs):
            column = slice((near + j) * width, (near + j + 1) * width)
            last += dot(rows_ref[0:total, column], late[...])
        lead = back_ref[:, 0:ff]
        swapped = flag_ref[0] != 0
        gate_part = sums_ref[:, 0:ff] + jnp.where(swapped, last, lead)
        up_part = sums_ref[:, ff : 2 * ff] + jnp.where(swapped, lead, last)
        sigmoid_gate = jax.nn.sigmoid(gate_part)
        activated = gate_part * sigmoid_gate
        hidden = (activated * up_part).astype(BF16)
        d_gate = back_hidden * up_part * sigmoid_gate * (1.0 + gate_part * (1.0 - sigmoid_gate))
        d_up = back_hidden * activated
        far_first = jnp.where(swapped, d_up, d_gate).astype(BF16)
        far_second = jnp.where(swapped, d_gate, d_up).astype(BF16)
        d_gate, d_up = d_gate.astype(BF16), d_up.astype(BF16)
        trio_ref[:, 0:ff] = hidden
        trio_ref[:, ff : 2 * ff] = d_gate
        trio_ref[:, 2 * ff :] = d_up
        for j in range(near + len(far_pieces)):
            column = slice(j * width, (j + 1) * width)
            if j < near:
                down = weight_refs[2 * j + 1]
                back = dot_last(d_gate, weight_refs[2 * j][0:width, :])
                back += dot_last(d_up, weight_refs[2 * j][width:, :])
            else:
                one, two, down = far_refs[j - near]
                back = dot_last(far_first, one[...]) + dot_last(far_second, two[...])
            out = dot(hidden, down[...]).astype(BF16)
            back = back.astype(BF16)
            for e in range(count):
                part = slice(e * capacity, (e + 1) * capacity)
                chunk_refs[e][0:capacity, column] = out[part]
                chunk_refs[e][capacity:, column] = back[part]

    outs = [shape((2 * capacity, model_width))] * count + [shape((total, 3 * ff))]
    got = call(kernel, outs, flag, rows, sums, far, *weights, smem=1)
    return got[:count], got[count]


def gradients(keeps, trios, width, ff):
    count = len(keeps)

    def kernel(*refs):
        keep_refs, trio_refs = refs[:count], refs[count : 2 * count]
        gate_ref, up_ref, down_ref = refs[2 * count :]
        half = keep_refs[0].shape[0] // 2
        x = jnp.concatenate([r[0:half, 0:width] for r in keep_refs], axis=0)
        dy = jnp.concatenate([r[half:, 0:width] for r in keep_refs], axis=0)
        trio = jnp.concatenate([r[...] for r in trio_refs], axis=0)
        gate_ref[...] = dot_first(x, trio[:, ff : 2 * ff]).astype(BF16)
        up_ref[...] = dot_first(x, trio[:, 2 * ff :]).astype(BF16)
        down_ref[...] = dot_first(trio[:, 0:ff], dy).astype(BF16)

    outs = [shape((width, ff)), shape((width, ff)), shape((ff, width))]
    return call(kernel, outs, *keeps, *trios)


def collect(place, ids, select, table, cotangent, chunks, dp_count, even):
    count = len(chunks)
    capacity = chunks[0].shape[0] // 2
    total = count * capacity
    token_rows, model_width = cotangent.shape
    width = model_width // dp_count

    def kernel(place_ref, ids_ref, select_ref, table_ref, dy_ref, *refs):
        chunk_refs, (mixed_ref, grad_ref, gates_ref) = refs[:count], refs[count:]
        inner = 0.0
        for j in range(dp_count):
            column = slice(j * width, (j + 1) * width)
            home = pl.ds(pl.multiple_of((place_ref[1] ^ j) * width, width), width)
            out = jnp.concatenate([r[0:capacity, column] for r in chunk_refs], axis=0)
            back = jnp.concatenate([r[capacity:, column] for r in chunk_refs], axis=0)
            mixed_ref[:, home] = dot(table_ref[...], jnp.concatenate([out] * 2, axis=0)).astype(BF16)
            grad_ref[:, home] = dot(table_ref[...], jnp.concatenate([back] * 2, axis=0)).astype(BF16)
            inner += dot_last(out, dy_ref[:, home])
        inner = jnp.where(select_ref[...] > 0, inner, 0.0)
        step = step_of(lax.broadcasted_iota(jnp.int32, (total, token_rows), 0) // capacity, count)
        far = step + place_ref[0]
        wanted = step ^ place_ref[0] if even else jnp.where(far >= count, far - count, far)
        for k in range(ids_ref.shape[0]):
            hit = ids_ref[k : k + 1, :] == wanted
            gates_ref[k : k + 1, :] = jnp.sum(jnp.where(hit, inner, 0.0), axis=0, keepdims=True)

    outs = [
        shape((token_rows, model_width)),
        shape((token_rows, model_width)),
        shape(ids.shape, F32),
    ]
    return call(
        kernel, outs, place, ids, select, table, cotangent, *chunks, smem=1, weight=COLLECT_WEIGHT
    )


def on_device(tokens, cotangent, expert_ids, gate_probs, w_gate, w_up, w_down):
    expert_count = lax.axis_size("expert")
    dp_count = lax.axis_size("dp")
    token_rows = tokens.shape[0]
    width, ff = w_gate.shape[1:]
    capacity = 2 * token_rows * expert_ids.shape[1] // EXPERTS
    group = lax.axis_index("groups").astype(jnp.int32)
    place = jnp.stack([lax.axis_index("expert"), lax.axis_index("dp")]).astype(jnp.int32)
    even = expert_count & (expert_count - 1) == 0
    paired = lax.axis_size("groups") == 2
    flag = (group if paired else jnp.zeros_like(group)).reshape(1)

    def to_dp(array, mask):
        return lax.ppermute(array, "dp", [(i, i ^ mask) for i in range(dp_count)])

    def to_group(array):
        return lax.ppermute(array, "groups", [(0, 1), (1, 0)])

    def to_expert(array, step):
        if even:
            pairs = [(i, i ^ step) for i in range(expert_count)]
        else:
            pairs = [(i, (i + step) % expert_count) for i in range(expert_count)]
        return lax.ppermute(array, "expert", pairs)

    def after(values, *others):
        return lax.optimization_barrier((values, others))[0]

    lead, both = choose(flag, w_gate[0], w_up[0])
    down = after(w_down[0], lead)
    masks = range(CORES, dp_count, CORES)
    lead_got = {mask: to_dp(lead, mask) for mask in masks}
    near_pieces = [(both, down), (to_dp(both, 1), to_dp(down, 1))]

    ids, probs = expert_ids.T, gate_probs.T
    send, select, table = slots(
        place, ids, probs, tokens, cotangent, expert_count, capacity, dp_count, even
    )
    send, down_far = after((send, down), near_pieces[1])
    down_got = {mask: to_dp(down_far, mask) for mask in masks}
    lead_got = after(lead_got, send)
    if paired:
        late_got = {mask: to_group(lead_got[mask]) for mask in masks}
    else:
        late_got = {mask: to_dp(w_up[0], mask) for mask in masks}
    ways = [step_of(i, expert_count) for i in range(expert_count)]
    got = [send[0]] + [to_expert(c, j) for c, j in zip(send[1:], ways[1:])]

    rows, parts = arrange(got, dp_count, CORES)
    lead_sib = {mask: to_dp(lead_got[mask], 1) for mask in masks}
    far_leads = [w for mask in masks for w in (lead_got[mask], None)]
    sums = first_half(rows, near_pieces, far_leads, width)
    late_got = after(late_got, sums)
    kept = [parts[0]] + [to_dp(parts[i + 1], mask) for i, mask in enumerate(masks)]
    far_pieces = []
    for mask in masks:
        late_sib, down_sib = to_dp(late_got[mask], 1), to_dp(down_got[mask], 1)
        far_pieces += [
            (lead_got[mask], late_got[mask], down_got[mask]),
            (lead_sib[mask], late_sib, down_sib),
        ]
    far = far_sums(
        rows,
        sums,
        [w for mask in masks for w in (None, lead_sib[mask])],
        [p[2] for p in far_pieces],
        CORES,
        width,
    )
    back, trio = second_half(
        flag, rows, sums, far, near_pieces, far_pieces, width, expert_count
    )

    home = [back[0]]
    home += [to_expert(c, j if even else -j) for c, j in zip(back[1:], ways[1:])]
    peers = [*masks, 1, *(mask + 1 for mask in masks)]
    trios = [trio] + [to_dp(trio, j) for j in peers]
    kept = after(kept, trios[2])
    theirs = to_dp(jnp.concatenate([k[:, width:] for k in kept], axis=0), 1)
    size = rows.shape[0]
    kept += [theirs[i * size : (i + 1) * size] for i in range(len(kept))]
    mixed, grad_tokens, grad_gates = collect(
        place, ids, select, table, cotangent, home, dp_count, even
    )
    mixed, kept, trios = lax.optimization_barrier((mixed, kept, trios))
    grad_w_gate, grad_w_up, grad_w_down = gradients(kept, trios, width, ff)
    return (
        mixed,
        grad_tokens,
        grad_gates.T,
        grad_w_gate[None],
        grad_w_up[None],
        grad_w_down[None],
    )


def solution(mesh):
    rows = P(("groups", "expert", "dp"), None)
    in_specs = (
        rows,
        rows,
        rows,
        rows,
        P("expert", "dp", None),
        P("expert", "dp", None),
        P("expert", None, "dp"),
    )
    out_specs = (
        rows,
        rows,
        rows,
        P(("groups", "expert"), "dp", None),
        P(("groups", "expert"), "dp", None),
        P(("groups", "expert"), None, "dp"),
    )
    return jax.shard_map(
        on_device, mesh=mesh, in_specs=in_specs, out_specs=out_specs, check_vma=False
    )
```

```python
import jax
import jax.numpy as jnp
from jax import lax
from jax.experimental import pallas as pl
from jax.experimental.pallas import tpu as pltpu
from jax.sharding import PartitionSpec as P

EXPERTS = 128
CORES = 2
BF16 = jnp.bfloat16
F32 = jnp.float32
VMEM_LIMIT = 16 << 20
FIRST_WEIGHT = 9 * 10**9
COLLECT_WEIGHT = 1 << 33
BACK_WEIGHT = 1 << 33
ARRANGE_WEIGHT = 3500 * 10**6


def dot(left, right):
    return jnp.dot(left, right, preferred_element_type=F32)


def dot_first(left, right):
    return lax.dot_general(left, right, (((0,), (0,)), ((), ())), preferred_element_type=F32)


def dot_last(left, right):
    return lax.dot_general(left, right, (((1,), (1,)), ((), ())), preferred_element_type=F32)


def shape(dims, dtype=BF16):
    return jax.ShapeDtypeStruct(dims, dtype)


def call(kernel, out_shape, *args, smem=0, scratch=(), anywhere=(), weight=1):
    vmem = pl.BlockSpec(memory_space=pltpu.VMEM)
    args = [
        pltpu.with_memory_space_constraint(a, pltpu.HBM) if i in anywhere else a
        for i, a in enumerate(args)
    ]
    specs = [
        pl.BlockSpec(memory_space=pltpu.SMEM)
        if i < smem
        else pl.BlockSpec(memory_space=pl.ANY)
        if i in anywhere
        else vmem
        for i in range(len(args))
    ]
    return pl.pallas_call(
        kernel,
        out_shape=out_shape,
        in_specs=specs,
        out_specs=jax.tree.map(lambda _: vmem, out_shape),
        scratch_shapes=list(scratch),
        compiler_params=pltpu.CompilerParams(vmem_limit_bytes=VMEM_LIMIT),
        cost_estimate=pl.CostEstimate(flops=weight, bytes_accessed=1, transcendentals=0),
    )(*args)


def step_of(index, count):
    step = 1 + (index + count // 2 - 2) % max(count - 1, 1)
    return jnp.where(index == 0, 0, step) if isinstance(index, jax.Array) else step * (index > 0)


def choose(flag, first, second):
    rows, columns = first.shape

    def kernel(flag_ref, first_ref, second_ref, one_ref, both_ref, sems):
        top = pltpu.make_async_copy(first_ref, both_ref.at[0:rows], sems.at[0])
        bottom = pltpu.make_async_copy(second_ref, both_ref.at[rows:], sems.at[1])
        top.start()
        bottom.start()

        @pl.when(flag_ref[0] == 0)
        def _():
            copy = pltpu.make_async_copy(first_ref, one_ref, sems.at[2])
            copy.start()
            copy.wait()

        @pl.when(flag_ref[0] != 0)
        def _():
            copy = pltpu.make_async_copy(second_ref, one_ref, sems.at[2])
            copy.start()
            copy.wait()

        top.wait()
        bottom.wait()

    return call(
        kernel,
        [shape((rows, columns)), shape((2 * rows, columns))],
        flag,
        first,
        second,
        smem=1,
        anywhere=(1, 2),
        scratch=[pltpu.SemaphoreType.DMA((3,))],
    )


def slots(place, ids, probs, tokens, cotangent, expert_count, capacity, dp_count, even):
    top_count, token_rows = ids.shape
    width = tokens.shape[1] // dp_count
    total = expert_count * capacity

    def kernel(place_ref, ids_ref, probs_ref, x_ref, dy_hbm, *outs):
        chunks, (select_ref, table_ref, dy_ref, sem) = outs[:expert_count], outs[expert_count:]
        fetch = pltpu.make_async_copy(dy_hbm, dy_ref, sem)
        fetch.start()
        row = lax.broadcasted_iota(jnp.int32, (total, token_rows), 0)
        step = step_of(row // capacity, expert_count)
        far = step + place_ref[0]
        wanted = step ^ place_ref[0] if even else jnp.where(far >= expert_count, far - expert_count, far)
        named = jnp.zeros((total, token_rows), F32)
        prob = jnp.zeros((total, token_rows), F32)
        for k in range(top_count):
            hit = ids_ref[k : k + 1, :] == wanted
            named = jnp.where(hit, 1.0, named)
            prob = jnp.where(hit, probs_ref[k : k + 1, :], prob)
        earlier = lax.broadcasted_iota(jnp.int32, (token_rows, token_rows), 0)
        later = lax.broadcasted_iota(jnp.int32, (token_rows, token_rows), 1)
        before = jnp.where(earlier < later, 1.0, 0.0).astype(BF16)
        slot = dot(named.astype(BF16), before)
        own_slot = (row % capacity).astype(F32)
        select = jnp.where((named > 0.5) & (slot == own_slot), 1.0, 0.0)
        pick = select.astype(BF16)
        select_ref[...] = pick
        def gather(ref, first):
            for j in range(dp_count):
                source = pl.ds(pl.multiple_of((place_ref[1] ^ j) * width, width), width)
                got = dot(pick, ref[:, source]).astype(BF16)
                for e in range(expert_count):
                    chunks[e][first : first + capacity, j * width : (j + 1) * width] = got[
                        e * capacity : (e + 1) * capacity
                    ]

        gather(x_ref, 0)
        table = (select * prob).T
        high = table.astype(BF16)
        table_ref[:, 0:total] = high
        table_ref[:, total:] = (table - high.astype(F32)).astype(BF16)
        fetch.wait()
        gather(dy_ref, capacity)

    outs = [shape((2 * capacity, tokens.shape[1]))] * expert_count
    outs += [shape((total, token_rows)), shape((token_rows, 2 * total))]
    got = call(
        kernel,
        outs,
        place,
        ids,
        probs,
        tokens,
        cotangent,
        smem=1,
        anywhere=(4,),
        scratch=[pltpu.VMEM(cotangent.shape, BF16), pltpu.SemaphoreType.DMA],
    )
    return got[:expert_count], got[expert_count], got[expert_count + 1]


def arrange(chunks, dp_count, near):
    count = len(chunks)
    capacity, model_width = chunks[0].shape[0] // 2, chunks[0].shape[1]
    total = count * capacity
    width = model_width // dp_count * near
    dp_count //= near

    def kernel(*refs):
        chunk_refs, rows_ref, part_refs = refs[:count], refs[count], refs[count + 1 :]
        for e in range(count):
            x, dy = slice(e * capacity, (e + 1) * capacity), slice(total + e * capacity, total + (e + 1) * capacity)
            rows_ref[x, :] = chunk_refs[e][0:capacity, :]
            rows_ref[dy, :] = chunk_refs[e][capacity:, :]
            for j in range(dp_count):
                column = slice(j * width, (j + 1) * width)
                part_refs[j][x, :] = chunk_refs[e][0:capacity, column]
                part_refs[j][dy, :] = chunk_refs[e][capacity:, column]

    outs = [shape((2 * total, model_width))] + [shape((2 * total, width))] * dp_count
    got = call(kernel, outs, *chunks, weight=ARRANGE_WEIGHT)
    return got[0], got[1:]


def first_half(rows, near_pieces, far_leads, width):
    total = rows.shape[0] // 2
    ff = near_pieces[0][1].shape[0]
    near = len(near_pieces)
    given = [(j, w) for j, w in enumerate(far_leads) if w is not None]
    weights = [w for p in near_pieces for w in p] + [w for _, w in given]

    def kernel(rows_ref, *refs):
        weight_refs, sums_ref = refs[:-1], refs[-1]
        sums = [0.0, 0.0, 0.0, 0.0]
        for j in range(near):
            column = slice(j * width, (j + 1) * width)
            x, dy = rows_ref[0:total, column], rows_ref[total:, column]
            sums[0] += dot(x, weight_refs[2 * j][0:width, :])
            sums[1] += dot(x, weight_refs[2 * j][width:, :])
            sums[3] += dot_last(dy, weight_refs[2 * j + 1][...])
        for i, (j, _) in enumerate(given):
            x = rows_ref[0:total, (near + j) * width : (near + j + 1) * width]
            sums[2] += dot(x, weight_refs[2 * near + i][...])
        for k in range(4):
            sums_ref[:, k * ff : (k + 1) * ff] = sums[k]

    return call(kernel, shape((total, 4 * ff), F32), rows, *weights, weight=FIRST_WEIGHT)


def far_sums(rows, sums, leads, downs, near, width):
    total = rows.shape[0] // 2
    ff = sums.shape[1] // 4
    given = [(j, w) for j, w in enumerate(leads) if w is not None]

    def kernel(rows_ref, sums_ref, *refs):
        lead_refs, down_refs, out_ref = refs[: len(given)], refs[len(given) : -1], refs[-1]
        lead = sums_ref[:, 2 * ff : 3 * ff]
        back_hidden = sums_ref[:, 3 * ff :]
        for (j, _), ref in zip(given, lead_refs):
            lead += dot(rows_ref[0:total, (near + j) * width : (near + j + 1) * width], ref[...])
        for j, ref in enumerate(down_refs):
            column = slice((near + j) * width, (near + j + 1) * width)
            back_hidden += dot_last(rows_ref[total:, column], ref[...])
        out_ref[:, 0:ff] = lead
        out_ref[:, ff:] = back_hidden

    return call(
        kernel,
        shape((total, 2 * ff), F32),
        rows,
        sums,
        *(w for _, w in given),
        *downs,
        weight=BACK_WEIGHT,
    )


def second_half(flag, rows, sums, far, near_pieces, far_pieces, width, count):
    total = rows.shape[0] // 2
    capacity = total // count
    model_width = rows.shape[1]
    ff = sums.shape[1] // 4
    near = len(near_pieces)
    weights = [w for p in (*near_pieces, *far_pieces) for w in p]

    def kernel(flag_ref, rows_ref, sums_ref, back_ref, *refs):
        weight_refs, outs = refs[: len(weights)], refs[len(weights) :]
        chunk_refs, trio_ref = outs[:count], outs[count]
        far_refs = [weight_refs[2 * near + 3 * j : 2 * near + 3 * j + 3] for j in range(len(far_pieces))]
        last, back_hidden = 0.0, back_ref[:, ff:]
        for j, (_, late, _) in enumerate(far_refs):
            column = slice((near + j) * width, (near + j + 1) * width)
            last += dot(rows_ref[0:total, column], late[...])
        lead = back_ref[:, 0:ff]
        swapped = flag_ref[0] != 0
        gate_part = sums_ref[:, 0:ff] + jnp.where(swapped, last, lead)
        up_part = sums_ref[:, ff : 2 * ff] + jnp.where(swapped, lead, last)
        sigmoid_gate = jax.nn.sigmoid(gate_part)
        activated = gate_part * sigmoid_gate
        hidden = (activated * up_part).astype(BF16)
        d_gate = back_hidden * up_part * sigmoid_gate * (1.0 + gate_part * (1.0 - sigmoid_gate))
        d_up = back_hidden * activated
        far_first = jnp.where(swapped, d_up, d_gate).astype(BF16)
        far_second = jnp.where(swapped, d_gate, d_up).astype(BF16)
        d_gate, d_up = d_gate.astype(BF16), d_up.astype(BF16)
        trio_ref[:, 0:ff] = hidden
        trio_ref[:, ff : 2 * ff] = d_gate
        trio_ref[:, 2 * ff :] = d_up
        for j in range(near + len(far_pieces)):
            column = slice(j * width, (j + 1) * width)
            if j < near:
                down = weight_refs[2 * j + 1]
                back = dot_last(d_gate, weight_refs[2 * j][0:width, :])
                back += dot_last(d_up, weight_refs[2 * j][width:, :])
            else:
                one, two, down = far_refs[j - near]
                back = dot_last(far_first, one[...]) + dot_last(far_second, two[...])
            out = dot(hidden, down[...]).astype(BF16)
            back = back.astype(BF16)
            for e in range(count):
                part = slice(e * capacity, (e + 1) * capacity)
                chunk_refs[e][0:capacity, column] = out[part]
                chunk_refs[e][capacity:, column] = back[part]

    outs = [shape((2 * capacity, model_width))] * count + [shape((total, 3 * ff))]
    got = call(kernel, outs, flag, rows, sums, far, *weights, smem=1)
    return got[:count], got[count]


def gradients(keeps, trios, width, ff):
    count = len(keeps)

    def kernel(*refs):
        keep_refs, trio_refs = refs[:count], refs[count : 2 * count]
        gate_ref, up_ref, down_ref = refs[2 * count :]
        half = keep_refs[0].shape[0] // 2
        x = jnp.concatenate([r[0:half, 0:width] for r in keep_refs], axis=0)
        dy = jnp.concatenate([r[half:, 0:width] for r in keep_refs], axis=0)
        trio = jnp.concatenate([r[...] for r in trio_refs], axis=0)
        gate_ref[...] = dot_first(x, trio[:, ff : 2 * ff]).astype(BF16)
        up_ref[...] = dot_first(x, trio[:, 2 * ff :]).astype(BF16)
        down_ref[...] = dot_first(trio[:, 0:ff], dy).astype(BF16)

    outs = [shape((width, ff)), shape((width, ff)), shape((ff, width))]
    return call(kernel, outs, *keeps, *trios)


def collect(place, ids, select, table, cotangent, chunks, dp_count, even):
    count = len(chunks)
    capacity = chunks[0].shape[0] // 2
    total = count * capacity
    token_rows, model_width = cotangent.shape
    width = model_width // dp_count

    def kernel(place_ref, ids_ref, select_ref, table_ref, dy_ref, *refs):
        chunk_refs, (mixed_ref, grad_ref, gates_ref) = refs[:count], refs[count:]
        out = jnp.concatenate([r[0:capacity, :] for r in chunk_refs], axis=0)
        back = jnp.concatenate([r[capacity:, :] for r in chunk_refs], axis=0)
        mixed = dot(table_ref[...], jnp.concatenate([out] * 2, axis=0)).astype(BF16)
        grad = dot(table_ref[...], jnp.concatenate([back] * 2, axis=0)).astype(BF16)
        inner = 0.0
        for j in range(dp_count):
            column = slice(j * width, (j + 1) * width)
            home = pl.ds(pl.multiple_of((place_ref[1] ^ j) * width, width), width)
            mixed_ref[:, home] = mixed[:, column]
            grad_ref[:, home] = grad[:, column]
            inner += dot_last(out[:, column], dy_ref[:, home])
        inner = jnp.where(select_ref[...] > 0, inner, 0.0)
        step = step_of(lax.broadcasted_iota(jnp.int32, (total, token_rows), 0) // capacity, count)
        far = step + place_ref[0]
        wanted = step ^ place_ref[0] if even else jnp.where(far >= count, far - count, far)
        for k in range(ids_ref.shape[0]):
            hit = ids_ref[k : k + 1, :] == wanted
            gates_ref[k : k + 1, :] = jnp.sum(jnp.where(hit, inner, 0.0), axis=0, keepdims=True)

    outs = [
        shape((token_rows, model_width)),
        shape((token_rows, model_width)),
        shape(ids.shape, F32),
    ]
    return call(
        kernel, outs, place, ids, select, table, cotangent, *chunks, smem=1, weight=COLLECT_WEIGHT
    )


def on_device(tokens, cotangent, expert_ids, gate_probs, w_gate, w_up, w_down):
    expert_count = lax.axis_size("expert")
    dp_count = lax.axis_size("dp")
    token_rows = tokens.shape[0]
    width, ff = w_gate.shape[1:]
    capacity = 2 * token_rows * expert_ids.shape[1] // EXPERTS
    group = lax.axis_index("groups").astype(jnp.int32)
    place = jnp.stack([lax.axis_index("expert"), lax.axis_index("dp")]).astype(jnp.int32)
    even = expert_count & (expert_count - 1) == 0
    paired = lax.axis_size("groups") == 2
    flag = (group if paired else jnp.zeros_like(group)).reshape(1)

    def to_dp(array, mask):
        return lax.ppermute(array, "dp", [(i, i ^ mask) for i in range(dp_count)])

    def to_group(array):
        return lax.ppermute(array, "groups", [(0, 1), (1, 0)])

    def to_expert(array, step):
        if even:
            pairs = [(i, i ^ step) for i in range(expert_count)]
        else:
            pairs = [(i, (i + step) % expert_count) for i in range(expert_count)]
        return lax.ppermute(array, "expert", pairs)

    def after(values, *others):
        return lax.optimization_barrier((values, others))[0]

    lead, both = choose(flag, w_gate[0], w_up[0])
    down = after(w_down[0], lead)
    masks = range(CORES, dp_count, CORES)
    lead_got = {mask: to_dp(lead, mask) for mask in masks}
    near_pieces = [(both, down), (to_dp(both, 1), to_dp(down, 1))]

    ids, probs = expert_ids.T, gate_probs.T
    send, select, table = slots(
        place, ids, probs, tokens, cotangent, expert_count, capacity, dp_count, even
    )
    send, down_far = after((send, down), near_pieces[1])
    down_got = {mask: to_dp(down_far, mask) for mask in masks}
    lead_got = after(lead_got, send)
    if paired:
        late_got = {mask: to_group(lead_got[mask]) for mask in masks}
    else:
        late_got = {mask: to_dp(w_up[0], mask) for mask in masks}
    ways = [step_of(i, expert_count) for i in range(expert_count)]
    got = [send[0]] + [to_expert(c, j) for c, j in zip(send[1:], ways[1:])]

    rows, parts = arrange(got, dp_count, CORES)
    lead_sib = {mask: to_dp(lead_got[mask], 1) for mask in masks}
    far_leads = [w for mask in masks for w in (lead_got[mask], None)]
    sums = first_half(rows, near_pieces, far_leads, width)
    late_got = after(late_got, sums)
    kept = [parts[0]] + [to_dp(parts[i + 1], mask) for i, mask in enumerate(masks)]
    far_pieces = []
    for mask in masks:
        late_sib, down_sib = to_dp(late_got[mask], 1), to_dp(down_got[mask], 1)
        far_pieces += [
            (lead_got[mask], late_got[mask], down_got[mask]),
            (lead_sib[mask], late_sib, down_sib),
        ]
    far = far_sums(
        rows,
        sums,
        [w for mask in masks for w in (None, lead_sib[mask])],
        [p[2] for p in far_pieces],
        CORES,
        width,
    )
    back, trio = second_half(
        flag, rows, sums, far, near_pieces, far_pieces, width, expert_count
    )

    home = [back[0]]
    home += [to_expert(c, j if even else -j) for c, j in zip(back[1:], ways[1:])]
    peers = [*masks, 1, *(mask + 1 for mask in masks)]
    trios = [trio] + [to_dp(trio, j) for j in peers]
    kept = after(kept, trios[2])
    theirs = to_dp(jnp.concatenate([k[:, width:] for k in kept], axis=0), 1)
    size = rows.shape[0]
    kept += [theirs[i * size : (i + 1) * size] for i in range(len(kept))]
    mixed, grad_tokens, grad_gates = collect(
        place, ids, select, table, cotangent, home, dp_count, even
    )
    mixed, kept, trios = lax.optimization_barrier((mixed, kept, trios))
    grad_w_gate, grad_w_up, grad_w_down = gradients(kept, trios, width, ff)
    return (
        mixed,
        grad_tokens,
        grad_gates.T,
        grad_w_gate[None],
        grad_w_up[None],
        grad_w_down[None],
    )


def solution(mesh):
    rows = P(("groups", "expert", "dp"), None)
    in_specs = (
        rows,
        rows,
        rows,
        rows,
        P("expert", "dp", None),
        P("expert", "dp", None),
        P("expert", None, "dp"),
    )
    out_specs = (
        rows,
        rows,
        rows,
        P(("groups", "expert"), "dp", None),
        P(("groups", "expert"), "dp", None),
        P(("groups", "expert"), None, "dp"),
    )
    return jax.shard_map(
        on_device, mesh=mesh, in_specs=in_specs, out_specs=out_specs, check_vma=False
    )
```

```python
import jax
import jax.numpy as jnp
from jax import lax
from jax.experimental import pallas as pl
from jax.experimental.pallas import tpu as pltpu
from jax.sharding import PartitionSpec as P

EXPERTS = 128
CORES = 2
BF16 = jnp.bfloat16
F32 = jnp.float32
VMEM_LIMIT = 16 << 20
FIRST_WEIGHT = 9 * 10**9
COLLECT_WEIGHT = 1 << 33
BACK_WEIGHT = 1 << 33
ARRANGE_WEIGHT = 3500 * 10**6


def dot(left, right):
    return jnp.dot(left, right, preferred_element_type=F32)


def dot_first(left, right):
    return lax.dot_general(left, right, (((0,), (0,)), ((), ())), preferred_element_type=F32)


def dot_last(left, right):
    return lax.dot_general(left, right, (((1,), (1,)), ((), ())), preferred_element_type=F32)


def shape(dims, dtype=BF16):
    return jax.ShapeDtypeStruct(dims, dtype)


def call(kernel, out_shape, *args, smem=0, scratch=(), anywhere=(), weight=1):
    vmem = pl.BlockSpec(memory_space=pltpu.VMEM)
    args = [
        pltpu.with_memory_space_constraint(a, pltpu.HBM) if i in anywhere else a
        for i, a in enumerate(args)
    ]
    specs = [
        pl.BlockSpec(memory_space=pltpu.SMEM)
        if i < smem
        else pl.BlockSpec(memory_space=pl.ANY)
        if i in anywhere
        else vmem
        for i in range(len(args))
    ]
    return pl.pallas_call(
        kernel,
        out_shape=out_shape,
        in_specs=specs,
        out_specs=jax.tree.map(lambda _: vmem, out_shape),
        scratch_shapes=list(scratch),
        compiler_params=pltpu.CompilerParams(vmem_limit_bytes=VMEM_LIMIT),
        cost_estimate=pl.CostEstimate(flops=weight, bytes_accessed=1, transcendentals=0),
    )(*args)


def step_of(index, count):
    step = 1 + (index + count // 2 - 2) % max(count - 1, 1)
    return jnp.where(index == 0, 0, step) if isinstance(index, jax.Array) else step * (index > 0)


def choose(flag, first, second, *small):
    rows, columns = first.shape

    def kernel(flag_ref, first_ref, second_ref, *refs):
        given, (one_ref, both_ref), rest = refs[: len(small)], refs[len(small) : len(small) + 2], refs[len(small) + 2 :]
        held, sems = rest[:-1], rest[-1]
        extra = [pltpu.make_async_copy(g, h, sems.at[3 + i]) for i, (g, h) in enumerate(zip(given, held))]
        for copy in extra:
            copy.start()
        top = pltpu.make_async_copy(first_ref, both_ref.at[0:rows], sems.at[0])
        bottom = pltpu.make_async_copy(second_ref, both_ref.at[rows:], sems.at[1])
        top.start()
        bottom.start()

        @pl.when(flag_ref[0] == 0)
        def _():
            copy = pltpu.make_async_copy(first_ref, one_ref, sems.at[2])
            copy.start()
            copy.wait()

        @pl.when(flag_ref[0] != 0)
        def _():
            copy = pltpu.make_async_copy(second_ref, one_ref, sems.at[2])
            copy.start()
            copy.wait()

        top.wait()
        bottom.wait()
        for copy in extra:
            copy.wait()

    return call(
        kernel,
        [shape((rows, columns)), shape((2 * rows, columns)), *(shape(a.shape, a.dtype) for a in small)],
        flag,
        first,
        second,
        *small,
        smem=1,
        anywhere=range(1, 3 + len(small)),
        scratch=[pltpu.SemaphoreType.DMA((3 + len(small),))],
    )


def slots(place, ids, probs, tokens, cotangent, expert_count, capacity, dp_count, even):
    top_count, token_rows = ids.shape
    width = tokens.shape[1] // dp_count
    total = expert_count * capacity

    def kernel(place_ref, ids_ref, probs_ref, x_ref, dy_hbm, *outs):
        chunks, (select_ref, table_ref, dy_ref, sem) = outs[:expert_count], outs[expert_count:]
        fetch = pltpu.make_async_copy(dy_hbm, dy_ref, sem)
        fetch.start()
        row = lax.broadcasted_iota(jnp.int32, (total, token_rows), 0)
        step = step_of(row // capacity, expert_count)
        far = step + place_ref[0]
        wanted = step ^ place_ref[0] if even else jnp.where(far >= expert_count, far - expert_count, far)
        named = jnp.zeros((total, token_rows), F32)
        prob = jnp.zeros((total, token_rows), F32)
        for k in range(top_count):
            hit = ids_ref[k : k + 1, :] == wanted
            named = jnp.where(hit, 1.0, named)
            prob = jnp.where(hit, probs_ref[k : k + 1, :], prob)
        earlier = lax.broadcasted_iota(jnp.int32, (token_rows, token_rows), 0)
        later = lax.broadcasted_iota(jnp.int32, (token_rows, token_rows), 1)
        before = jnp.where(earlier < later, 1.0, 0.0).astype(BF16)
        slot = dot(named.astype(BF16), before)
        own_slot = (row % capacity).astype(F32)
        select = jnp.where((named > 0.5) & (slot == own_slot), 1.0, 0.0)
        pick = select.astype(BF16)
        select_ref[...] = pick
        def gather(ref, first):
            for j in range(dp_count):
                source = pl.ds(pl.multiple_of((place_ref[1] ^ j) * width, width), width)
                got = dot(pick, ref[:, source]).astype(BF16)
                for e in range(expert_count):
                    chunks[e][first : first + capacity, j * width : (j + 1) * width] = got[
                        e * capacity : (e + 1) * capacity
                    ]

        gather(x_ref, 0)
        table = (select * prob).T
        high = table.astype(BF16)
        table_ref[:, 0:total] = high
        table_ref[:, total:] = (table - high.astype(F32)).astype(BF16)
        fetch.wait()
        gather(dy_ref, capacity)

    outs = [shape((2 * capacity, tokens.shape[1]))] * expert_count
    outs += [shape((total, token_rows)), shape((token_rows, 2 * total))]
    got = call(
        kernel,
        outs,
        place,
        ids,
        probs,
        tokens,
        cotangent,
        smem=1,
        anywhere=(4,),
        scratch=[pltpu.VMEM(cotangent.shape, BF16), pltpu.SemaphoreType.DMA],
    )
    return got[:expert_count], got[expert_count], got[expert_count + 1]


def arrange(chunks, dp_count, near):
    count = len(chunks)
    capacity, model_width = chunks[0].shape[0] // 2, chunks[0].shape[1]
    total = count * capacity
    width = model_width // dp_count * near
    dp_count //= near

    def kernel(*refs):
        chunk_refs, rows_ref, part_refs = refs[:count], refs[count], refs[count + 1 :]
        for e in range(count):
            x, dy = slice(e * capacity, (e + 1) * capacity), slice(total + e * capacity, total + (e + 1) * capacity)
            rows_ref[x, :] = chunk_refs[e][0:capacity, :]
            rows_ref[dy, :] = chunk_refs[e][capacity:, :]
            for j in range(dp_count):
                column = slice(j * width, (j + 1) * width)
                part_refs[j][x, :] = chunk_refs[e][0:capacity, column]
                part_refs[j][dy, :] = chunk_refs[e][capacity:, column]

    outs = [shape((2 * total, model_width))] + [shape((2 * total, width))] * dp_count
    got = call(kernel, outs, *chunks, weight=ARRANGE_WEIGHT)
    return got[0], got[1:]


def first_half(rows, near_pieces, far_leads, width):
    total = rows.shape[0] // 2
    ff = near_pieces[0][1].shape[0]
    near = len(near_pieces)
    given = [(j, w) for j, w in enumerate(far_leads) if w is not None]
    weights = [w for p in near_pieces for w in p] + [w for _, w in given]

    def kernel(rows_ref, *refs):
        weight_refs, sums_ref = refs[:-1], refs[-1]
        sums = [0.0, 0.0, 0.0, 0.0]
        for j in range(near):
            column = slice(j * width, (j + 1) * width)
            x, dy = rows_ref[0:total, column], rows_ref[total:, column]
            sums[0] += dot(x, weight_refs[2 * j][0:width, :])
            sums[1] += dot(x, weight_refs[2 * j][width:, :])
            sums[3] += dot_last(dy, weight_refs[2 * j + 1][...])
        for i, (j, _) in enumerate(given):
            x = rows_ref[0:total, (near + j) * width : (near + j + 1) * width]
            sums[2] += dot(x, weight_refs[2 * near + i][...])
        for k in range(4):
            sums_ref[:, k * ff : (k + 1) * ff] = sums[k]

    return call(kernel, shape((total, 4 * ff), F32), rows, *weights, weight=FIRST_WEIGHT)


def far_sums(rows, sums, leads, downs, near, width):
    total = rows.shape[0] // 2
    ff = sums.shape[1] // 4
    given = [(j, w) for j, w in enumerate(leads) if w is not None]

    def kernel(rows_ref, sums_ref, *refs):
        lead_refs, down_refs, out_ref = refs[: len(given)], refs[len(given) : -1], refs[-1]
        lead = sums_ref[:, 2 * ff : 3 * ff]
        back_hidden = sums_ref[:, 3 * ff :]
        for (j, _), ref in zip(given, lead_refs):
            lead += dot(rows_ref[0:total, (near + j) * width : (near + j + 1) * width], ref[...])
        for j, ref in enumerate(down_refs):
            column = slice((near + j) * width, (near + j + 1) * width)
            back_hidden += dot_last(rows_ref[total:, column], ref[...])
        out_ref[:, 0:ff] = lead
        out_ref[:, ff:] = back_hidden

    return call(
        kernel,
        shape((total, 2 * ff), F32),
        rows,
        sums,
        *(w for _, w in given),
        *downs,
        weight=BACK_WEIGHT,
    )


def second_half(flag, rows, sums, far, near_pieces, far_pieces, width, count):
    total = rows.shape[0] // 2
    capacity = total // count
    model_width = rows.shape[1]
    ff = sums.shape[1] // 4
    near = len(near_pieces)
    weights = [w for p in (*near_pieces, *far_pieces) for w in p]

    def kernel(flag_ref, rows_ref, sums_ref, back_ref, *refs):
        weight_refs, outs = refs[: len(weights)], refs[len(weights) :]
        chunk_refs, trio_ref = outs[:count], outs[count]
        far_refs = [weight_refs[2 * near + 3 * j : 2 * near + 3 * j + 3] for j in range(len(far_pieces))]
        last, back_hidden = 0.0, back_ref[:, ff:]
        for j, (_, late, _) in enumerate(far_refs):
            column = slice((near + j) * width, (near + j + 1) * width)
            last += dot(rows_ref[0:total, column], late[...])
        lead = back_ref[:, 0:ff]
        swapped = flag_ref[0] != 0
        gate_part = sums_ref[:, 0:ff] + jnp.where(swapped, last, lead)
        up_part = sums_ref[:, ff : 2 * ff] + jnp.where(swapped, lead, last)
        sigmoid_gate = jax.nn.sigmoid(gate_part)
        activated = gate_part * sigmoid_gate
        hidden = (activated * up_part).astype(BF16)
        d_gate = back_hidden * up_part * sigmoid_gate * (1.0 + gate_part * (1.0 - sigmoid_gate))
        d_up = back_hidden * activated
        far_first = jnp.where(swapped, d_up, d_gate).astype(BF16)
        far_second = jnp.where(swapped, d_gate, d_up).astype(BF16)
        d_gate, d_up = d_gate.astype(BF16), d_up.astype(BF16)
        trio_ref[:, 0:ff] = hidden
        trio_ref[:, ff : 2 * ff] = d_gate
        trio_ref[:, 2 * ff :] = d_up
        for j in range(near + len(far_pieces)):
            column = slice(j * width, (j + 1) * width)
            if j < near:
                down = weight_refs[2 * j + 1]
                back = dot_last(d_gate, weight_refs[2 * j][0:width, :])
                back += dot_last(d_up, weight_refs[2 * j][width:, :])
            else:
                one, two, down = far_refs[j - near]
                back = dot_last(far_first, one[...]) + dot_last(far_second, two[...])
            out = dot(hidden, down[...]).astype(BF16)
            back = back.astype(BF16)
            for e in range(count):
                part = slice(e * capacity, (e + 1) * capacity)
                chunk_refs[e][0:capacity, column] = out[part]
                chunk_refs[e][capacity:, column] = back[part]

    outs = [shape((2 * capacity, model_width))] * count + [shape((total, 3 * ff))]
    got = call(kernel, outs, flag, rows, sums, far, *weights, smem=1)
    return got[:count], got[count]


def gradients(keeps, trios, width, ff):
    count = len(keeps)

    def kernel(*refs):
        keep_refs, trio_refs = refs[:count], refs[count : 2 * count]
        gate_ref, up_ref, down_ref = refs[2 * count :]
        half = keep_refs[0].shape[0] // 2
        x = jnp.concatenate([r[0:half, 0:width] for r in keep_refs], axis=0)
        dy = jnp.concatenate([r[half:, 0:width] for r in keep_refs], axis=0)
        trio = jnp.concatenate([r[...] for r in trio_refs], axis=0)
        gate_ref[...] = dot_first(x, trio[:, ff : 2 * ff]).astype(BF16)
        up_ref[...] = dot_first(x, trio[:, 2 * ff :]).astype(BF16)
        down_ref[...] = dot_first(trio[:, 0:ff], dy).astype(BF16)

    outs = [shape((width, ff)), shape((width, ff)), shape((ff, width))]
    return call(kernel, outs, *keeps, *trios)


def collect(place, ids, select, table, cotangent, chunks, dp_count, even):
    count = len(chunks)
    capacity = chunks[0].shape[0] // 2
    total = count * capacity
    token_rows, model_width = cotangent.shape
    width = model_width // dp_count

    def kernel(place_ref, ids_ref, select_ref, table_ref, dy_ref, *refs):
        chunk_refs, (mixed_ref, grad_ref, gates_ref) = refs[:count], refs[count:]
        out = jnp.concatenate([r[0:capacity, :] for r in chunk_refs], axis=0)
        back = jnp.concatenate([r[capacity:, :] for r in chunk_refs], axis=0)
        mixed = dot(table_ref[...], jnp.concatenate([out] * 2, axis=0)).astype(BF16)
        grad = dot(table_ref[...], jnp.concatenate([back] * 2, axis=0)).astype(BF16)
        inner = 0.0
        for j in range(dp_count):
            column = slice(j * width, (j + 1) * width)
            home = pl.ds(pl.multiple_of((place_ref[1] ^ j) * width, width), width)
            mixed_ref[:, home] = mixed[:, column]
            grad_ref[:, home] = grad[:, column]
            inner += dot_last(out[:, column], dy_ref[:, home])
        inner = jnp.where(select_ref[...] > 0, inner, 0.0)
        step = step_of(lax.broadcasted_iota(jnp.int32, (total, token_rows), 0) // capacity, count)
        far = step + place_ref[0]
        wanted = step ^ place_ref[0] if even else jnp.where(far >= count, far - count, far)
        for k in range(ids_ref.shape[0]):
            hit = ids_ref[k : k + 1, :] == wanted
            gates_ref[k : k + 1, :] = jnp.sum(jnp.where(hit, inner, 0.0), axis=0, keepdims=True)

    outs = [
        shape((token_rows, model_width)),
        shape((token_rows, model_width)),
        shape(ids.shape, F32),
    ]
    return call(
        kernel, outs, place, ids, select, table, cotangent, *chunks, smem=1, weight=COLLECT_WEIGHT
    )


def on_device(tokens, cotangent, expert_ids, gate_probs, w_gate, w_up, w_down):
    expert_count = lax.axis_size("expert")
    dp_count = lax.axis_size("dp")
    token_rows = tokens.shape[0]
    width, ff = w_gate.shape[1:]
    capacity = 2 * token_rows * expert_ids.shape[1] // EXPERTS
    group = lax.axis_index("groups").astype(jnp.int32)
    place = jnp.stack([lax.axis_index("expert"), lax.axis_index("dp")]).astype(jnp.int32)
    even = expert_count & (expert_count - 1) == 0
    paired = lax.axis_size("groups") == 2
    flag = (group if paired else jnp.zeros_like(group)).reshape(1)

    def to_dp(array, mask):
        return lax.ppermute(array, "dp", [(i, i ^ mask) for i in range(dp_count)])

    def to_group(array):
        return lax.ppermute(array, "groups", [(0, 1), (1, 0)])

    def to_expert(array, step):
        if even:
            pairs = [(i, i ^ step) for i in range(expert_count)]
        else:
            pairs = [(i, (i + step) % expert_count) for i in range(expert_count)]
        return lax.ppermute(array, "expert", pairs)

    def after(values, *others):
        return lax.optimization_barrier((values, others))[0]

    lead, both, ids, probs = choose(flag, w_gate[0], w_up[0], expert_ids.T, gate_probs.T)
    down = after(w_down[0], lead)
    masks = range(CORES, dp_count, CORES)
    lead_got = {mask: to_dp(lead, mask) for mask in masks}
    near_pieces = [(both, down), (to_dp(both, 1), to_dp(down, 1))]

    send, select, table = slots(
        place, ids, probs, tokens, cotangent, expert_count, capacity, dp_count, even
    )
    send, down_far = after((send, down), near_pieces[1])
    down_got = {mask: to_dp(down_far, mask) for mask in masks}
    lead_got = after(lead_got, send)
    if paired:
        late_got = {mask: to_group(lead_got[mask]) for mask in masks}
    else:
        late_got = {mask: to_dp(w_up[0], mask) for mask in masks}
    ways = [step_of(i, expert_count) for i in range(expert_count)]
    got = [send[0]] + [to_expert(c, j) for c, j in zip(send[1:], ways[1:])]

    rows, parts = arrange(got, dp_count, CORES)
    lead_sib = {mask: to_dp(lead_got[mask], 1) for mask in masks}
    far_leads = [w for mask in masks for w in (lead_got[mask], None)]
    sums = first_half(rows, near_pieces, far_leads, width)
    late_got = after(late_got, sums)
    kept = [parts[0]] + [to_dp(parts[i + 1], mask) for i, mask in enumerate(masks)]
    far_pieces = []
    for mask in masks:
        late_sib, down_sib = to_dp(late_got[mask], 1), to_dp(down_got[mask], 1)
        far_pieces += [
            (lead_got[mask], late_got[mask], down_got[mask]),
            (lead_sib[mask], late_sib, down_sib),
        ]
    far = far_sums(
        rows,
        sums,
        [w for mask in masks for w in (None, lead_sib[mask])],
        [p[2] for p in far_pieces],
        CORES,
        width,
    )
    back, trio = second_half(
        flag, rows, sums, far, near_pieces, far_pieces, width, expert_count
    )

    home = [back[0]]
    home += [to_expert(c, j if even else -j) for c, j in zip(back[1:], ways[1:])]
    peers = [*masks, 1, *(mask + 1 for mask in masks)]
    trios = [trio] + [to_dp(trio, j) for j in peers]
    kept = after(kept, trios[2])
    theirs = to_dp(jnp.concatenate([k[:, width:] for k in kept], axis=0), 1)
    size = rows.shape[0]
    kept += [theirs[i * size : (i + 1) * size] for i in range(len(kept))]
    mixed, grad_tokens, grad_gates = collect(
        place, ids, select, table, cotangent, home, dp_count, even
    )
    mixed, kept, trios = lax.optimization_barrier((mixed, kept, trios))
    grad_w_gate, grad_w_up, grad_w_down = gradients(kept, trios, width, ff)
    return (
        mixed,
        grad_tokens,
        grad_gates.T,
        grad_w_gate[None],
        grad_w_up[None],
        grad_w_down[None],
    )


def solution(mesh):
    rows = P(("groups", "expert", "dp"), None)
    in_specs = (
        rows,
        rows,
        rows,
        rows,
        P("expert", "dp", None),
        P("expert", "dp", None),
        P("expert", None, "dp"),
    )
    out_specs = (
        rows,
        rows,
        rows,
        P(("groups", "expert"), "dp", None),
        P(("groups", "expert"), "dp", None),
        P(("groups", "expert"), None, "dp"),
    )
    return jax.shard_map(
        on_device, mesh=mesh, in_specs=in_specs, out_specs=out_specs, check_vma=False
    )
```

```python
import jax
import jax.numpy as jnp
from jax import lax
from jax.experimental import pallas as pl
from jax.experimental.pallas import tpu as pltpu
from jax.sharding import PartitionSpec as P

EXPERTS = 128
CORES = 2
BF16 = jnp.bfloat16
F32 = jnp.float32
VMEM_LIMIT = 16 << 20
FIRST_WEIGHT = 9 * 10**9
COLLECT_WEIGHT = 1 << 33
BACK_WEIGHT = 10**9
ARRANGE_WEIGHT = 3500 * 10**6


def dot(left, right):
    return jnp.dot(left, right, preferred_element_type=F32)


def dot_first(left, right):
    return lax.dot_general(left, right, (((0,), (0,)), ((), ())), preferred_element_type=F32)


def dot_last(left, right):
    return lax.dot_general(left, right, (((1,), (1,)), ((), ())), preferred_element_type=F32)


def shape(dims, dtype=BF16):
    return jax.ShapeDtypeStruct(dims, dtype)


def call(kernel, out_shape, *args, smem=0, scratch=(), anywhere=(), weight=1):
    vmem = pl.BlockSpec(memory_space=pltpu.VMEM)
    args = [
        pltpu.with_memory_space_constraint(a, pltpu.HBM) if i in anywhere else a
        for i, a in enumerate(args)
    ]
    specs = [
        pl.BlockSpec(memory_space=pltpu.SMEM)
        if i < smem
        else pl.BlockSpec(memory_space=pl.ANY)
        if i in anywhere
        else vmem
        for i in range(len(args))
    ]
    return pl.pallas_call(
        kernel,
        out_shape=out_shape,
        in_specs=specs,
        out_specs=jax.tree.map(lambda _: vmem, out_shape),
        scratch_shapes=list(scratch),
        compiler_params=pltpu.CompilerParams(vmem_limit_bytes=VMEM_LIMIT),
        cost_estimate=pl.CostEstimate(flops=weight, bytes_accessed=1, transcendentals=0),
    )(*args)


def step_of(index, count):
    step = 1 + (index + count // 2 - 2) % max(count - 1, 1)
    return jnp.where(index == 0, 0, step) if isinstance(index, jax.Array) else step * (index > 0)


def choose(flag, first, second):
    rows, columns = first.shape

    def kernel(flag_ref, first_ref, second_ref, one_ref, both_ref, sems):
        top = pltpu.make_async_copy(first_ref, both_ref.at[0:rows], sems.at[0])
        bottom = pltpu.make_async_copy(second_ref, both_ref.at[rows:], sems.at[1])
        top.start()
        bottom.start()

        @pl.when(flag_ref[0] == 0)
        def _():
            copy = pltpu.make_async_copy(first_ref, one_ref, sems.at[2])
            copy.start()
            copy.wait()

        @pl.when(flag_ref[0] != 0)
        def _():
            copy = pltpu.make_async_copy(second_ref, one_ref, sems.at[2])
            copy.start()
            copy.wait()

        top.wait()
        bottom.wait()

    return call(
        kernel,
        [shape((rows, columns)), shape((2 * rows, columns))],
        flag,
        first,
        second,
        smem=1,
        anywhere=(1, 2),
        scratch=[pltpu.SemaphoreType.DMA((3,))],
    )


def slots(place, ids, probs, tokens, cotangent, expert_count, capacity, dp_count, even):
    top_count, token_rows = ids.shape
    width = tokens.shape[1] // dp_count
    total = expert_count * capacity

    def kernel(place_ref, ids_ref, probs_ref, x_ref, dy_hbm, *outs):
        chunks, (select_ref, table_ref, dy_ref, sem) = outs[:expert_count], outs[expert_count:]
        fetch = pltpu.make_async_copy(dy_hbm, dy_ref, sem)
        fetch.start()
        row = lax.broadcasted_iota(jnp.int32, (total, token_rows), 0)
        step = step_of(row // capacity, expert_count)
        far = step + place_ref[0]
        wanted = step ^ place_ref[0] if even else jnp.where(far >= expert_count, far - expert_count, far)
        named = jnp.zeros((total, token_rows), F32)
        prob = jnp.zeros((total, token_rows), F32)
        for k in range(top_count):
            hit = ids_ref[k : k + 1, :] == wanted
            named = jnp.where(hit, 1.0, named)
            prob = jnp.where(hit, probs_ref[k : k + 1, :], prob)
        earlier = lax.broadcasted_iota(jnp.int32, (token_rows, token_rows), 0)
        later = lax.broadcasted_iota(jnp.int32, (token_rows, token_rows), 1)
        before = jnp.where(earlier < later, 1.0, 0.0).astype(BF16)
        slot = dot(named.astype(BF16), before)
        own_slot = (row % capacity).astype(F32)
        select = jnp.where((named > 0.5) & (slot == own_slot), 1.0, 0.0)
        pick = select.astype(BF16)
        select_ref[...] = pick
        def gather(ref, first):
            for j in range(dp_count):
                source = pl.ds(pl.multiple_of((place_ref[1] ^ j) * width, width), width)
                got = dot(pick, ref[:, source]).astype(BF16)
                for e in range(expert_count):
                    chunks[e][first : first + capacity, j * width : (j + 1) * width] = got[
                        e * capacity : (e + 1) * capacity
                    ]

        gather(x_ref, 0)
        table = (select * prob).T
        high = table.astype(BF16)
        table_ref[:, 0:total] = high
        table_ref[:, total:] = (table - high.astype(F32)).astype(BF16)
        fetch.wait()
        gather(dy_ref, capacity)

    outs = [shape((2 * capacity, tokens.shape[1]))] * expert_count
    outs += [shape((total, token_rows)), shape((token_rows, 2 * total))]
    got = call(
        kernel,
        outs,
        place,
        ids,
        probs,
        tokens,
        cotangent,
        smem=1,
        anywhere=(4,),
        scratch=[pltpu.VMEM(cotangent.shape, BF16), pltpu.SemaphoreType.DMA],
    )
    return got[:expert_count], got[expert_count], got[expert_count + 1]


def arrange(chunks, dp_count, near):
    count = len(chunks)
    capacity, model_width = chunks[0].shape[0] // 2, chunks[0].shape[1]
    total = count * capacity
    width = model_width // dp_count * near
    dp_count //= near

    def kernel(*refs):
        chunk_refs, rows_ref, part_refs = refs[:count], refs[count], refs[count + 1 :]
        for e in range(count):
            x, dy = slice(e * capacity, (e + 1) * capacity), slice(total + e * capacity, total + (e + 1) * capacity)
            rows_ref[x, :] = chunk_refs[e][0:capacity, :]
            rows_ref[dy, :] = chunk_refs[e][capacity:, :]
            for j in range(dp_count):
                column = slice(j * width, (j + 1) * width)
                part_refs[j][x, :] = chunk_refs[e][0:capacity, column]
                part_refs[j][dy, :] = chunk_refs[e][capacity:, column]

    outs = [shape((2 * total, model_width))] + [shape((2 * total, width))] * dp_count
    got = call(kernel, outs, *chunks, weight=ARRANGE_WEIGHT)
    return got[0], got[1:]


def first_half(rows, near_pieces, far_leads, width):
    total = rows.shape[0] // 2
    ff = near_pieces[0][1].shape[0]
    near = len(near_pieces)
    given = [(j, w) for j, w in enumerate(far_leads) if w is not None]
    weights = [w for p in near_pieces for w in p] + [w for _, w in given]

    def kernel(rows_ref, *refs):
        weight_refs, sums_ref = refs[:-1], refs[-1]
        sums = [0.0, 0.0, 0.0, 0.0]
        for j in range(near):
            column = slice(j * width, (j + 1) * width)
            x, dy = rows_ref[0:total, column], rows_ref[total:, column]
            sums[0] += dot(x, weight_refs[2 * j][0:width, :])
            sums[1] += dot(x, weight_refs[2 * j][width:, :])
            sums[3] += dot_last(dy, weight_refs[2 * j + 1][...])
        for i, (j, _) in enumerate(given):
            x = rows_ref[0:total, (near + j) * width : (near + j + 1) * width]
            sums[2] += dot(x, weight_refs[2 * near + i][...])
        for k in range(4):
            sums_ref[:, k * ff : (k + 1) * ff] = sums[k]

    return call(kernel, shape((total, 4 * ff), F32), rows, *weights, weight=FIRST_WEIGHT)


def far_sums(rows, sums, leads, downs, near, width):
    total = rows.shape[0] // 2
    ff = sums.shape[1] // 4
    given = [(j, w) for j, w in enumerate(leads) if w is not None]

    def kernel(rows_ref, sums_ref, *refs):
        lead_refs, down_refs, out_ref = refs[: len(given)], refs[len(given) : -1], refs[-1]
        lead = sums_ref[:, 2 * ff : 3 * ff]
        back_hidden = sums_ref[:, 3 * ff :]
        for (j, _), ref in zip(given, lead_refs):
            lead += dot(rows_ref[0:total, (near + j) * width : (near + j + 1) * width], ref[...])
        for j, ref in enumerate(down_refs):
            column = slice((near + j) * width, (near + j + 1) * width)
            back_hidden += dot_last(rows_ref[total:, column], ref[...])
        out_ref[:, 0:ff] = lead
        out_ref[:, ff:] = back_hidden

    return call(
        kernel,
        shape((total, 2 * ff), F32),
        rows,
        sums,
        *(w for _, w in given),
        *downs,
        weight=BACK_WEIGHT,
    )


def second_half(flag, rows, sums, far, near_pieces, far_pieces, width, count):
    total = rows.shape[0] // 2
    capacity = total // count
    model_width = rows.shape[1]
    ff = sums.shape[1] // 4
    near = len(near_pieces)
    weights = [w for p in (*near_pieces, *far_pieces) for w in p]

    def kernel(flag_ref, rows_ref, sums_ref, back_ref, *refs):
        weight_refs, outs = refs[: len(weights)], refs[len(weights) :]
        chunk_refs, trio_ref = outs[:count], outs[count]
        far_refs = [weight_refs[2 * near + 3 * j : 2 * near + 3 * j + 3] for j in range(len(far_pieces))]
        last, back_hidden = 0.0, back_ref[:, ff:]
        for j, (_, late, _) in enumerate(far_refs):
            column = slice((near + j) * width, (near + j + 1) * width)
            last += dot(rows_ref[0:total, column], late[...])
        lead = back_ref[:, 0:ff]
        swapped = flag_ref[0] != 0
        gate_part = sums_ref[:, 0:ff] + jnp.where(swapped, last, lead)
        up_part = sums_ref[:, ff : 2 * ff] + jnp.where(swapped, lead, last)
        sigmoid_gate = jax.nn.sigmoid(gate_part)
        activated = gate_part * sigmoid_gate
        hidden = (activated * up_part).astype(BF16)
        d_gate = back_hidden * up_part * sigmoid_gate * (1.0 + gate_part * (1.0 - sigmoid_gate))
        d_up = back_hidden * activated
        far_first = jnp.where(swapped, d_up, d_gate).astype(BF16)
        far_second = jnp.where(swapped, d_gate, d_up).astype(BF16)
        d_gate, d_up = d_gate.astype(BF16), d_up.astype(BF16)
        trio_ref[:, 0:ff] = hidden
        trio_ref[:, ff : 2 * ff] = d_gate
        trio_ref[:, 2 * ff :] = d_up
        for j in range(near + len(far_pieces)):
            column = slice(j * width, (j + 1) * width)
            if j < near:
                down = weight_refs[2 * j + 1]
                back = dot_last(d_gate, weight_refs[2 * j][0:width, :])
                back += dot_last(d_up, weight_refs[2 * j][width:, :])
            else:
                one, two, down = far_refs[j - near]
                back = dot_last(far_first, one[...]) + dot_last(far_second, two[...])
            out = dot(hidden, down[...]).astype(BF16)
            back = back.astype(BF16)
            for e in range(count):
                part = slice(e * capacity, (e + 1) * capacity)
                chunk_refs[e][0:capacity, column] = out[part]
                chunk_refs[e][capacity:, column] = back[part]

    outs = [shape((2 * capacity, model_width))] * count + [shape((total, 3 * ff))]
    got = call(kernel, outs, flag, rows, sums, far, *weights, smem=1)
    return got[:count], got[count]


def gradients(keeps, trios, width, ff):
    count = len(keeps)

    def kernel(*refs):
        keep_refs, trio_refs = refs[:count], refs[count : 2 * count]
        gate_ref, up_ref, down_ref = refs[2 * count :]
        half = keep_refs[0].shape[0] // 2
        x = jnp.concatenate([r[0:half, 0:width] for r in keep_refs], axis=0)
        dy = jnp.concatenate([r[half:, 0:width] for r in keep_refs], axis=0)
        trio = jnp.concatenate([r[...] for r in trio_refs], axis=0)
        gate_ref[...] = dot_first(x, trio[:, ff : 2 * ff]).astype(BF16)
        up_ref[...] = dot_first(x, trio[:, 2 * ff :]).astype(BF16)
        down_ref[...] = dot_first(trio[:, 0:ff], dy).astype(BF16)

    outs = [shape((width, ff)), shape((width, ff)), shape((ff, width))]
    return call(kernel, outs, *keeps, *trios)


def collect(place, ids, select, table, cotangent, chunks, dp_count, even):
    count = len(chunks)
    capacity = chunks[0].shape[0] // 2
    total = count * capacity
    token_rows, model_width = cotangent.shape
    width = model_width // dp_count

    def kernel(place_ref, ids_ref, select_ref, table_ref, dy_ref, *refs):
        chunk_refs, (mixed_ref, grad_ref, gates_ref) = refs[:count], refs[count:]
        out = jnp.concatenate([r[0:capacity, :] for r in chunk_refs], axis=0)
        back = jnp.concatenate([r[capacity:, :] for r in chunk_refs], axis=0)
        mixed = dot(table_ref[...], jnp.concatenate([out] * 2, axis=0)).astype(BF16)
        grad = dot(table_ref[...], jnp.concatenate([back] * 2, axis=0)).astype(BF16)
        inner = 0.0
        for j in range(dp_count):
            column = slice(j * width, (j + 1) * width)
            home = pl.ds(pl.multiple_of((place_ref[1] ^ j) * width, width), width)
            mixed_ref[:, home] = mixed[:, column]
            grad_ref[:, home] = grad[:, column]
            inner += dot_last(out[:, column], dy_ref[:, home])
        inner = jnp.where(select_ref[...] > 0, inner, 0.0)
        step = step_of(lax.broadcasted_iota(jnp.int32, (total, token_rows), 0) // capacity, count)
        far = step + place_ref[0]
        wanted = step ^ place_ref[0] if even else jnp.where(far >= count, far - count, far)
        for k in range(ids_ref.shape[0]):
            hit = ids_ref[k : k + 1, :] == wanted
            gates_ref[k : k + 1, :] = jnp.sum(jnp.where(hit, inner, 0.0), axis=0, keepdims=True)

    outs = [
        shape((token_rows, model_width)),
        shape((token_rows, model_width)),
        shape(ids.shape, F32),
    ]
    return call(
        kernel, outs, place, ids, select, table, cotangent, *chunks, smem=1, weight=COLLECT_WEIGHT
    )


def on_device(tokens, cotangent, expert_ids, gate_probs, w_gate, w_up, w_down):
    expert_count = lax.axis_size("expert")
    dp_count = lax.axis_size("dp")
    token_rows = tokens.shape[0]
    width, ff = w_gate.shape[1:]
    capacity = 2 * token_rows * expert_ids.shape[1] // EXPERTS
    group = lax.axis_index("groups").astype(jnp.int32)
    place = jnp.stack([lax.axis_index("expert"), lax.axis_index("dp")]).astype(jnp.int32)
    even = expert_count & (expert_count - 1) == 0
    paired = lax.axis_size("groups") == 2
    flag = (group if paired else jnp.zeros_like(group)).reshape(1)

    def to_dp(array, mask):
        return lax.ppermute(array, "dp", [(i, i ^ mask) for i in range(dp_count)])

    def to_group(array):
        return lax.ppermute(array, "groups", [(0, 1), (1, 0)])

    def to_expert(array, step):
        if even:
            pairs = [(i, i ^ step) for i in range(expert_count)]
        else:
            pairs = [(i, (i + step) % expert_count) for i in range(expert_count)]
        return lax.ppermute(array, "expert", pairs)

    def after(values, *others):
        return lax.optimization_barrier((values, others))[0]

    lead, both = choose(flag, w_gate[0], w_up[0])
    down = after(w_down[0], lead)
    masks = range(CORES, dp_count, CORES)
    lead_got = {mask: to_dp(lead, mask) for mask in masks}
    near_pieces = [(both, down), (to_dp(both, 1), to_dp(down, 1))]

    ids, probs = expert_ids.T, gate_probs.T
    send, select, table = slots(
        place, ids, probs, tokens, cotangent, expert_count, capacity, dp_count, even
    )
    send, down_far = after((send, down), near_pieces[1])
    down_got = {mask: to_dp(down_far, mask) for mask in masks}
    lead_got = after(lead_got, send)
    if paired:
        late_got = {mask: to_group(lead_got[mask]) for mask in masks}
    else:
        late_got = {mask: to_dp(w_up[0], mask) for mask in masks}
    ways = [step_of(i, expert_count) for i in range(expert_count)]
    got = [send[0]] + [to_expert(c, j) for c, j in zip(send[1:], ways[1:])]

    rows, parts = arrange(got, dp_count, CORES)
    lead_sib = {mask: to_dp(lead_got[mask], 1) for mask in masks}
    far_leads = [w for mask in masks for w in (lead_got[mask], None)]
    sums = first_half(rows, near_pieces, far_leads, width)
    late_got = after(late_got, sums)
    kept = [parts[0]] + [to_dp(parts[i + 1], mask) for i, mask in enumerate(masks)]
    far_pieces = []
    for mask in masks:
        late_sib, down_sib = to_dp(late_got[mask], 1), to_dp(down_got[mask], 1)
        far_pieces += [
            (lead_got[mask], late_got[mask], down_got[mask]),
            (lead_sib[mask], late_sib, down_sib),
        ]
    far = far_sums(
        rows,
        sums,
        [w for mask in masks for w in (None, lead_sib[mask])],
        [p[2] for p in far_pieces],
        CORES,
        width,
    )
    back, trio = second_half(
        flag, rows, sums, far, near_pieces, far_pieces, width, expert_count
    )

    home = [back[0]]
    home += [to_expert(c, j if even else -j) for c, j in zip(back[1:], ways[1:])]
    peers = [*masks, 1, *(mask + 1 for mask in masks)]
    trios = [trio] + [to_dp(trio, j) for j in peers]
    kept = after(kept, trios[2])
    theirs = to_dp(jnp.concatenate([k[:, width:] for k in kept], axis=0), 1)
    size = rows.shape[0]
    kept += [theirs[i * size : (i + 1) * size] for i in range(len(kept))]
    mixed, grad_tokens, grad_gates = collect(
        place, ids, select, table, cotangent, home, dp_count, even
    )
    mixed, kept, trios = lax.optimization_barrier((mixed, kept, trios))
    grad_w_gate, grad_w_up, grad_w_down = gradients(kept, trios, width, ff)
    return (
        mixed,
        grad_tokens,
        grad_gates.T,
        grad_w_gate[None],
        grad_w_up[None],
        grad_w_down[None],
    )


def solution(mesh):
    rows = P(("groups", "expert", "dp"), None)
    in_specs = (
        rows,
        rows,
        rows,
        rows,
        P("expert", "dp", None),
        P("expert", "dp", None),
        P("expert", None, "dp"),
    )
    out_specs = (
        rows,
        rows,
        rows,
        P(("groups", "expert"), "dp", None),
        P(("groups", "expert"), "dp", None),
        P(("groups", "expert"), None, "dp"),
    )
    return jax.shard_map(
        on_device, mesh=mesh, in_specs=in_specs, out_specs=out_specs, check_vma=False
    )
```
